32 devices in a mesh: groups: 2 (over y), cache: 4 (over z), fsdp: 2 (over x), head: 2 (over core).
Axes of the slice: x: 2, y: 2, z: 4, core: 2. Of those that a mesh axis runs over, the one named last changes fastest.
Arguments:
- tokens: bfloat16 [1024, 3072], P(('groups', 'cache')), parts along dimension 0, may hold values from -6 to 6
- norm_gain: float32 [3072], replicated, may hold values from 0.1 to 1.9
- w_query: bfloat16 [3072, 4096], P('cache', ('fsdp', 'head')), may hold values from -0.109375 to 0.109375
- w_key: bfloat16 [3072, 4096], P('cache', ('fsdp', 'head')), may hold values from -0.109375 to 0.109375
- w_value: bfloat16 [3072, 4096], P('cache', ('fsdp', 'head')), may hold values from -0.109375 to 0.109375
- w_out: bfloat16 [4096, 3072], P(('fsdp', 'head'), 'cache'), may hold values from -0.09375 to 0.09375
- query_gain: float32 [128], replicated, may hold values from 0.1 to 1.9
- key_gain: float32 [128], replicated, may hold values from 0.1 to 1.9
- cache_keys: bfloat16 [4096, 4096], P(('groups', 'cache'), ('fsdp', 'head')), parts along dimension 0, may hold values from -3 to 3
- cache_values: bfloat16 [4096, 4096], P(('groups', 'cache'), ('fsdp', 'head')), parts along dimension 0, may hold values from -6 to 6
- step_gate: float32 [2, 3072], replicated, may hold values from 2 to 16
- block_list: int32 [8, 4], P('groups'), parts along dimension 0, may hold values from 0 to 7, as said below
- block_home: int32 [16], P('groups'), parts along dimension 0, may hold values from 0 to 7, as said below
- reader_span: int32 [8], P('groups'), parts along dimension 0, may hold values from 0 to 3, as said below
Outputs:
- denoised: bfloat16 [1024, 3072], P(('groups', 'cache'), ('fsdp', 'head')), parts along dimension 0
The draws below stay inside these ranges and needn't reach their ends.
There are 2 independent parts, one for each index of `groups`. The reference program is written for one: setup_inputs(seed, part) draws one part's arguments, and reference() takes and returns one part's arrays. A program takes and returns all parts, laid end to end along the dimension named above; an argument that names none is the same for every part. Nothing has to cross between parts.
Inputs may be any that keep to these rules, and one draw needn't show every extreme that they name: A permutation of the storage slots: block b is held by cache device block_home[b] // 2. `block_list`: each row names 4 different blocks: blocks 0 to 1, then 2 window blocks, the one at position 2 + i being congruent to 2 + i modulo 4; the blocks of one row are held by different cache devices. `reader_span`: every span is named by 1 tiles.
All inputs are finite; a program needn't handle non-finite values.
Results may differ from the reference program's by a relative error of at most 0.023.
Values may be sent and summed in bfloat16 or wider, within the bound.
No kernel may reach another device: no remote copies, remote signals or barrier semaphores. Data moves between devices by JAX's collectives and lax.ppermute only.
A program may use at most 128 MiB of HBM per device.

```python
import math
import jax
import jax.numpy as jnp
from jax import lax

D = 3072
HEADS = 32
HEAD_DIM = 128
BLOCK = 256
ITERS = 2
SPANS = 4
SINKS = 2
TT = 128
BLK_DEV = 2
READERS = 4
WIN = 2
LIST = 4
TOKENS = 512
NBLK = 8
HD = 4096


def block_layout(key):
    sink_base = jax.random.permutation(jax.random.fold_in(key, 101), READERS).astype(jnp.int32)
    rest_order = jax.random.permutation(jax.random.fold_in(key, 202), READERS - SINKS)
    column_owner = jnp.concatenate([sink_base[:SINKS], sink_base[SINKS:][rest_order]]).astype(jnp.int32)
    owners = jnp.broadcast_to(column_owner[None, :], (BLK_DEV, READERS))
    place_keys = jax.random.split(jax.random.fold_in(key, 303), READERS)

    def owner_places(place_key):
        return jax.random.permutation(place_key, BLK_DEV).astype(jnp.int32)
    places = jax.vmap(owner_places)(place_keys)
    stripe_rows = jnp.broadcast_to(jnp.arange(BLK_DEV, dtype=jnp.int32)[:, None], (BLK_DEV, READERS))
    local_pos = places[owners, stripe_rows]
    home_slot = (owners * BLK_DEV + local_pos).reshape(NBLK).astype(jnp.int32)
    stripes = jax.random.randint(jax.random.fold_in(key, 404), (SPANS, WIN), 0, BLK_DEV).astype(jnp.int32)
    stripes = stripes.at[0, WIN - 1].set(BLK_DEV - 1)
    window = stripes * READERS + SINKS + jnp.arange(WIN, dtype=jnp.int32)[None, :]
    sink_ids = jnp.broadcast_to(jnp.arange(SINKS, dtype=jnp.int32)[None, :], (SPANS, SINKS))
    block_rows = jnp.concatenate([sink_ids, window.astype(jnp.int32)], axis=1)
    return (home_slot, block_rows)


def draw_block_home(key, part):
    return block_layout(key)[0]


def draw_block_list(key, part):
    return block_layout(key)[1]


def draw_reader_span(key, part):
    order = jax.random.permutation(jax.random.fold_in(key, 606), READERS)
    return (order % SPANS).astype(jnp.int32)


def level_of(stream_key, extent, cuts, least, high):
    factor_of, own = 1.0, jax.random.fold_in(stream_key, 6)
    for axis_at, blocks in cuts:
        draws = jnp.exp(jax.random.uniform(jax.random.fold_in(own, axis_at), (blocks,), jnp.float32, least / len(cuts), high / len(cuts)))
        factor_of = factor_of * jnp.repeat(draws, extent[axis_at] // blocks).reshape([-1 if axis == axis_at else 1 for axis in range(len(extent))])
    return factor_of


def noise(own_key, dims, width, limit, pieces=(), held_as=jnp.bfloat16):
    entries = jax.random.normal(own_key, dims, jnp.float32) * width
    if len(pieces) > 0:
        entries = level_of(own_key, dims, pieces, -0.22, 0.18) * entries
    return jnp.clip(entries, min=-limit, max=limit).astype(held_as)


def setup_inputs(seed: int = 0, part: int = 0) -> dict:
    seeds = jax.random.split(jax.random.key(seed), 15)
    part_keys = jax.random.split(jax.random.fold_in(seeds[14], part), 15)
    return {
        "tokens": noise(part_keys[0], (TOKENS, D), 1.0, 6.0, ((0, 4),)),
        "norm_gain": jnp.clip(1.0 + 0.18 * jax.random.normal(seeds[1], (D,), jnp.float32), 0.1, 1.9),
        "w_query": noise(seeds[2], (D, HD), D ** -0.5, 0.109375, ((0, 4), (1, 4))),
        "w_key": noise(seeds[3], (D, HD), D ** -0.5, 0.109375, ((0, 4), (1, 4))),
        "w_value": noise(seeds[4], (D, HD), D ** -0.5, 0.109375, ((0, 4), (1, 4))),
        "w_out": noise(seeds[5], (HD, D), HD ** -0.5, 0.09375, ((0, 4), (1, 4))),
        "query_gain": jnp.clip(1.0 + 0.18 * jax.random.normal(seeds[6], (HEAD_DIM,), jnp.float32), 0.1, 1.9),
        "key_gain": jnp.clip(1.0 + 0.18 * jax.random.normal(seeds[7], (HEAD_DIM,), jnp.float32), 0.1, 1.9),
        "cache_keys": noise(part_keys[8], (NBLK * BLOCK, HD), 1.0, 3.0, ((0, 4), (1, 4))),
        "cache_values": noise(part_keys[9], (NBLK * BLOCK, HD), 1.0, 6.0, ((0, 4), (1, 4))),
        "step_gate": jnp.clip(jnp.exp(jax.random.uniform(seeds[10], (ITERS, D), jnp.float32, math.log(2.0), math.log(16.0))), 2.0, 16.0),
        "block_list": draw_block_list(jax.random.fold_in(jax.random.fold_in(seeds[14], part), 71), part),
        "block_home": draw_block_home(jax.random.fold_in(jax.random.fold_in(seeds[14], part), 71), part),
        "reader_span": draw_reader_span(jax.random.fold_in(jax.random.fold_in(seeds[14], part), 71), part),
    }


epsilon = 1e-06

def rms_scale(values, gain_row):
    mean_square = lax.optimization_barrier(jnp.mean(values * values, axis=-1, keepdims=True))
    return values * lax.rsqrt(mean_square + epsilon) * gain_row

def head_norm(projected, gain_row):
    row_count = projected.shape[0]
    split = projected.reshape(row_count, -1, gain_row.shape[0])
    return rms_scale(split, gain_row).astype(jnp.bfloat16).reshape(row_count, -1)

def reference(tokens, norm_gain, w_query, w_key, w_value, w_out, query_gain, key_gain, cache_keys, cache_values, step_gate, block_list, block_home, reader_span):
    key_blocks = cache_keys.reshape(NBLK, BLOCK, HD)
    value_blocks = cache_values.reshape(NBLK, BLOCK, HD)
    score_scale = HEAD_DIM ** (-0.5)
    current = tokens
    for step_index in range(ITERS):
        normed = rms_scale(current.astype(jnp.float32), norm_gain).astype(jnp.bfloat16)
        queries = head_norm(jnp.dot(normed, w_query, preferred_element_type=jnp.float32), query_gain)
        own_keys = head_norm(jnp.dot(normed, w_key, preferred_element_type=jnp.float32), key_gain)
        own_values = jnp.dot(normed, w_value, preferred_element_type=jnp.float32).astype(jnp.bfloat16)

        def tile_attend(tile_index):
            start = (tile_index * TT).astype(jnp.int32)
            tile_query = lax.dynamic_slice_in_dim(queries, start, TT, 0)
            tile_key = lax.dynamic_slice_in_dim(own_keys, start, TT, 0)
            tile_value = lax.dynamic_slice_in_dim(own_values, start, TT, 0)
            span_index = jnp.take(reader_span, tile_index)
            picked = jnp.take(block_home, jnp.take(block_list, span_index, axis=0))
            key_rows = jnp.concatenate([jnp.take(key_blocks, picked, axis=0).reshape(LIST * BLOCK, HD), tile_key], axis=0)
            value_rows = jnp.concatenate([jnp.take(value_blocks, picked, axis=0).reshape(LIST * BLOCK, HD), tile_value], axis=0)
            query_heads = tile_query.astype(jnp.float32).reshape(TT, HEADS, HEAD_DIM)
            key_heads = key_rows.astype(jnp.float32).reshape(-1, HEADS, HEAD_DIM)
            value_heads = value_rows.astype(jnp.float32).reshape(-1, HEADS, HEAD_DIM)
            scores = jnp.einsum('qhd,khd->hqk', query_heads, key_heads, precision=lax.Precision.HIGHEST) * score_scale
            weights = jnp.exp(scores)
            totals = lax.optimization_barrier(jnp.sum(weights, axis=2))
            rounded = lax.optimization_barrier(weights.astype(jnp.bfloat16)).astype(jnp.float32)
            summed = jnp.einsum('hqk,khd->qhd', rounded, value_heads, precision=lax.Precision.HIGHEST)
            return (summed / jnp.transpose(totals)[:, :, None]).astype(jnp.bfloat16).reshape(TT, HD)
        mixed = lax.map(tile_attend, jnp.arange(READERS, dtype=jnp.int32)).reshape(TOKENS, HD)
        update = jnp.dot(mixed, w_out, preferred_element_type=jnp.float32)
        current = (current.astype(jnp.float32) + step_gate[step_index] * update).astype(jnp.bfloat16)
    return current
```

```python
import functools

import jax
import jax.numpy as jnp
from jax import lax
from jax.experimental import pallas as pl
from jax.experimental.pallas import tpu as pltpu
from jax.sharding import PartitionSpec as P

BLOCK = 256
ITERS = 2


epsilon = 1e-06


def rms_scale(values, gain_row):
    mean_square = jnp.mean(values * values, axis=-1, keepdims=True)
    return values * lax.rsqrt(mean_square + epsilon) * gain_row


def head_norm(projected, gain_row):
    row_count = projected.shape[0]
    split = projected.reshape(row_count, -1, gain_row.shape[0])
    return rms_scale(split, gain_row).astype(jnp.bfloat16).reshape(row_count, -1)


def attend(queries, key_rows, value_rows, head_dim):
    row_count = queries.shape[0]
    head_count = queries.shape[1] // head_dim
    query_heads = queries.reshape(row_count, head_count, head_dim)
    key_heads = key_rows.reshape(-1, head_count, head_dim)
    value_heads = value_rows.reshape(-1, head_count, head_dim)
    scores = jnp.einsum(
        "qhd,khd->hqk", query_heads, key_heads, preferred_element_type=jnp.float32
    ) * head_dim ** (-0.5)
    weights = jnp.exp(scores)
    totals = jnp.sum(weights, axis=2)
    summed = jnp.einsum(
        "hqk,khd->qhd",
        weights.astype(jnp.bfloat16),
        value_heads,
        preferred_element_type=jnp.float32,
    )
    return (
        (summed / jnp.transpose(totals)[:, :, None])
        .astype(jnp.bfloat16)
        .reshape(row_count, head_count * head_dim)
    )


def gathered_panels(
    tokens,
    norm_gain,
    w_query,
    w_key,
    w_value,
    w_out,
    query_gain,
    key_gain,
    cache_keys,
    cache_values,
    step_gate,
    block_list,
    block_home,
    reader_span,
):
    reader_index = lax.axis_index("cache")
    group_index = lax.axis_index(("fsdp", "head"))
    head_dim = query_gain.shape[0]
    panel_width = cache_keys.shape[1]
    held_blocks = cache_keys.shape[0] // BLOCK
    full_query, full_key, full_value = (
        lax.all_gather(w_query, "cache", axis=0, tiled=True),
        lax.all_gather(w_key, "cache", axis=0, tiled=True),
        lax.all_gather(w_value, "cache", axis=0, tiled=True),
    )
    out_panel = lax.all_gather(w_out, "cache", axis=1, tiled=True)
    wanted = jnp.take(block_list, reader_span, axis=0)
    home_slots = jnp.take(block_home, wanted)
    is_mine = home_slots // held_blocks == reader_index
    local_pos = jnp.sum(jnp.where(is_mine, home_slots % held_blocks, 0), axis=1)
    key_blocks = cache_keys.reshape(held_blocks, BLOCK, panel_width)
    value_blocks = cache_values.reshape(held_blocks, BLOCK, panel_width)
    send_keys = jnp.take(key_blocks, local_pos, axis=0)
    send_values = jnp.take(value_blocks, local_pos, axis=0)
    got_keys, got_values = (
        lax.all_to_all(send_keys, "cache", split_axis=0, concat_axis=0, tiled=True),
        lax.all_to_all(send_values, "cache", split_axis=0, concat_axis=0, tiled=True),
    )
    my_span = jnp.take(reader_span, reader_index)
    my_owners = jnp.take(block_home, jnp.take(block_list, my_span, axis=0)) // held_blocks
    fetched_keys = jnp.take(got_keys, my_owners, axis=0).reshape(-1, panel_width)
    fetched_values = jnp.take(got_values, my_owners, axis=0).reshape(-1, panel_width)
    out_columns = lax.all_to_all(
        out_panel, ("fsdp", "head"), split_axis=1, concat_axis=0, tiled=True
    )
    column_count = tokens.shape[1] // lax.axis_size(("fsdp", "head"))
    column_start = group_index * column_count
    current = tokens
    x_share = lax.dynamic_slice_in_dim(tokens, column_start, column_count, 1)
    for step_index in range(ITERS):
        normed = rms_scale(current.astype(jnp.float32), norm_gain).astype(jnp.bfloat16)
        queries = head_norm(
            jnp.dot(normed, full_query, preferred_element_type=jnp.float32), query_gain
        )
        own_keys = head_norm(
            jnp.dot(normed, full_key, preferred_element_type=jnp.float32), key_gain
        )
        own_values = jnp.dot(normed, full_value, preferred_element_type=jnp.float32).astype(
            jnp.bfloat16
        )
        all_keys = jnp.concatenate([fetched_keys, own_keys], axis=0)
        all_values = jnp.concatenate([fetched_values, own_values], axis=0)
        mixed = attend(queries, all_keys, all_values, head_dim)
        step_scale = step_gate[step_index]
        share_scale = lax.dynamic_slice_in_dim(step_scale, column_start, column_count, 0)
        heads_all = lax.all_gather(mixed, ("fsdp", "head"), axis=1, tiled=True)
        update = jnp.dot(heads_all, out_columns, preferred_element_type=jnp.float32)
        x_share = (x_share.astype(jnp.float32) + share_scale * update).astype(jnp.bfloat16)
        if step_index + 1 < ITERS:
            current = lax.all_gather(x_share, ("fsdp", "head"), axis=1, tiled=True)
    return x_share


WAYS = 4
VMEM_LIMIT = 56 * 1024 * 1024


def whole_specs(count):
    return [pl.BlockSpec(memory_space=pltpu.VMEM) for _ in range(count)]


def project_kernel(gain_ref, query_gain_ref, key_gain_ref, *refs):
    pieces, panels = refs[:WAYS], refs[WAYS : 3 * WAYS]
    q_ref, k_ref, v_ref, normed_ref = refs[3 * WAYS :]
    tile, width = pieces[0].shape[1:]
    for r in range(WAYS):
        rows = [pieces[r ^ k][k].astype(jnp.float32) for k in range(WAYS)]
        square = sum(jnp.sum(x * x, axis=-1, keepdims=True) for x in rows)
        scale = lax.rsqrt(square / (WAYS * width) + epsilon)
        for k in range(WAYS):
            normed_ref[k, r * tile : (r + 1) * tile, :] = (
                rows[k] * scale * gain_ref[k : k + 1, :]
            ).astype(jnp.bfloat16)
    head_dim = query_gain_ref.shape[1]
    for h in range(2):
        total = jnp.dot(normed_ref[0], panels[h][...], preferred_element_type=jnp.float32)
        for k in range(1, WAYS):
            total += jnp.dot(
                normed_ref[k], panels[2 * k + h][...], preferred_element_type=jnp.float32
            )
        lanes = slice(h * head_dim, (h + 1) * head_dim)
        q_ref[:, lanes] = rms_scale(total[:, :head_dim], query_gain_ref[...]).astype(jnp.bfloat16)
        k_ref[:, lanes] = rms_scale(
            total[:, head_dim : 2 * head_dim], key_gain_ref[...]
        ).astype(jnp.bfloat16)
        v_ref[:, lanes] = total[:, 2 * head_dim :].astype(jnp.bfloat16)


def project(pieces, panels, gain_rows, query_gain, key_gain):
    tile, width = pieces[0].shape[1:]
    head_dim = query_gain.shape[1]
    shape = jax.ShapeDtypeStruct((WAYS * tile, 2 * head_dim), jnp.bfloat16)
    return pl.pallas_call(
        project_kernel,
        out_shape=[shape] * 3,
        in_specs=whole_specs(3 + 3 * WAYS),
        out_specs=whole_specs(3),
        scratch_shapes=[pltpu.VMEM((WAYS, WAYS * tile, width), jnp.bfloat16)],
        compiler_params=pltpu.CompilerParams(vmem_limit_bytes=VMEM_LIMIT),
    )(gain_rows, query_gain, key_gain, *pieces, *panels)


def attend_kernel(pos_ref, q_ref, k_ref, v_ref, *refs):
    held, mixed_ref = refs[:WAYS], refs[WAYS]
    head_dim = q_ref.shape[1] // 2
    tile = q_ref.shape[0] // WAYS
    across = (((1,), (1,)), ((), ()))
    for r in range(WAYS):
        rows = slice(r * tile, (r + 1) * tile)
        for h in range(2):
            lanes = slice(h * head_dim, (h + 1) * head_dim)
            value_lanes = slice((2 + h) * head_dim, (3 + h) * head_dim)
            query = q_ref[rows, lanes]
            keys = [k_ref[rows, lanes]]
            values = [v_ref[rows, lanes]]
            for k in range(WAYS):
                start = pl.multiple_of(pos_ref[r * WAYS + k] * BLOCK, BLOCK)
                keys.append(held[k][pl.ds(start, BLOCK), lanes])
                values.append(held[k][pl.ds(start, BLOCK), value_lanes])
            total = jnp.zeros((tile, 1), jnp.float32)
            summed = jnp.zeros((tile, head_dim), jnp.float32)
            for key, value in zip(keys, values):
                scores = lax.dot_general(query, key, across, preferred_element_type=jnp.float32)
                weights = jnp.exp(scores * head_dim ** (-0.5))
                total += jnp.sum(weights, axis=-1, keepdims=True)
                summed += jnp.dot(
                    weights.astype(jnp.bfloat16), value, preferred_element_type=jnp.float32
                )
            mixed_ref[rows, lanes] = (summed / total).astype(jnp.bfloat16)


def attend_all(pos, q, k, v, held):
    return pl.pallas_call(
        attend_kernel,
        out_shape=jax.ShapeDtypeStruct(q.shape, jnp.bfloat16),
        in_specs=[pl.BlockSpec(memory_space=pltpu.SMEM)] + whole_specs(3 + WAYS),
        out_specs=pl.BlockSpec(memory_space=pltpu.VMEM),
        compiler_params=pltpu.CompilerParams(vmem_limit_bytes=VMEM_LIMIT),
    )(pos, q, k, v, *held)


def out_kernel(w_ref, *refs):
    mixed, (keep_ref, send_ref) = refs[:WAYS], refs[WAYS:]
    depth = mixed[0].shape[1]
    tile = mixed[0].shape[0] // WAYS
    for r in range(WAYS):
        row = jnp.concatenate(
            [mixed[k][(r ^ k) * tile : ((r ^ k) + 1) * tile, :] for k in range(WAYS)], axis=1
        )
        update = jnp.dot(row, w_ref[...], preferred_element_type=jnp.float32)
        rows = slice((r // 2) * tile, (r // 2 + 1) * tile)
        if r % 2 == 0:
            keep_ref[rows, :] = update
        else:
            send_ref[rows, :] = update.astype(jnp.bfloat16)


def project_out(w_rows, mixed):
    tile = mixed[0].shape[0] // WAYS
    width = w_rows.shape[1]
    return pl.pallas_call(
        out_kernel,
        out_shape=[
            jax.ShapeDtypeStruct((2 * tile, width), jnp.float32),
            jax.ShapeDtypeStruct((2 * tile, width), jnp.bfloat16),
        ],
        in_specs=whole_specs(1 + WAYS),
        out_specs=whole_specs(2),
        compiler_params=pltpu.CompilerParams(vmem_limit_bytes=VMEM_LIMIT),
    )(w_rows, *mixed)


SWAP = [(0, 1), (1, 0)]


def from_z(value, k):
    return lax.ppermute(value, "cache", [(i, i ^ k) for i in range(WAYS)])


def split_heads(
    tokens,
    norm_gain,
    w_query,
    w_key,
    w_value,
    w_out,
    query_gain,
    key_gain,
    cache_keys,
    cache_values,
    step_gate,
    block_list,
    block_home,
    reader_span,
):
    z = lax.axis_index("cache")
    p = lax.axis_index(("fsdp", "head"))
    y = lax.axis_index("groups")
    head_dim = query_gain.shape[0]
    held_blocks = cache_keys.shape[0] // BLOCK
    width = tokens.shape[1] // WAYS
    tile = tokens.shape[0]
    ways = jnp.arange(WAYS, dtype=jnp.int32)

    def head_of(array, k, h):
        return lax.dynamic_slice_in_dim(array, ((z ^ k) * 2 + (y ^ h)) * head_dim, head_dim, 1)

    def panel_of(k, h):
        return jnp.concatenate([head_of(w, k, h) for w in (w_query, w_key, w_value)], axis=1)

    def cache_of(k):
        return jnp.concatenate([head_of(a, k, h) for a in (cache_keys, cache_values) for h in (0, 1)], axis=1)

    piece = lax.dynamic_slice_in_dim(tokens, p * width, width, 1)
    by_z = jnp.stack([piece] + [from_z(piece, k) for k in range(1, WAYS)])
    by_x = jnp.stack([by_z, lax.ppermute(by_z, "fsdp", SWAP)])
    by_core = lax.ppermute(by_x, "head", SWAP)
    gathered = jnp.stack([by_x, by_core], axis=1).reshape(WAYS * WAYS, tile, width)

    near = [panel_of(0, 0)] + [from_z(panel_of(k, 0), k) for k in range(1, WAYS)]
    far = [panel_of(0, 1)] + [lax.ppermute(near[k], "groups", SWAP) for k in range(1, WAYS)]
    panels = [panel for pair in zip(near, far) for panel in pair]
    held = [cache_of(0)] + [from_z(cache_of(k), k) for k in range(1, WAYS)]

    source = (z ^ p ^ ways)[None, :] * WAYS + (p ^ ways[:, None] ^ ways[None, :])
    pieces = [jnp.take(gathered, source[j], axis=0) for j in range(WAYS)]
    x_share = pieces[0][0]

    gain_rows = jnp.take(norm_gain.reshape(WAYS, width), z ^ ways, axis=0)
    heads = jnp.stack([(z ^ ways) * 2 + y, (z ^ ways) * 2 + 1 - y], axis=1).reshape(-1)
    w_rows = jnp.take(w_out.reshape(2 * WAYS, head_dim, width), heads, axis=0).reshape(-1, width)
    gates = lax.dynamic_slice_in_dim(step_gate, z * width, width, 1)
    slots = jnp.take(block_home, jnp.take(block_list, jnp.take(reader_span, z ^ p ^ ways), axis=0))
    from_k = slots[:, :, None] // held_blocks == (z ^ ways)[None, None, :]
    pos = jnp.sum(jnp.where(from_k, (slots % held_blocks)[:, :, None], 0), axis=1).reshape(-1)

    for step in range(ITERS):
        q, k, v = project(pieces, panels, gain_rows, query_gain[None], key_gain[None])
        own = attend_all(pos, q, k, v, held)
        mixed = [own] + [from_z(own, k) for k in range(1, WAYS)]
        keep, send = project_out(w_rows, mixed)
        half = keep + lax.ppermute(send, "head", SWAP).astype(jnp.float32)
        other = lax.ppermute(half[tile:].astype(jnp.bfloat16), "fsdp", SWAP)
        update = half[:tile] + other.astype(jnp.float32)
        x_share = (x_share.astype(jnp.float32) + gates[step] * update).astype(jnp.bfloat16)
        if step + 1 < ITERS:
            by_z = jnp.stack([x_share] + [from_z(x_share, k) for k in range(1, WAYS)])
            by_x = lax.ppermute(by_z, "fsdp", SWAP)
            pieces = [
                by_z,
                lax.ppermute(by_z, "head", SWAP),
                by_x,
                lax.ppermute(by_x, "head", SWAP),
            ]
    moves = [
        (a * WAYS + b, (a ^ b) * WAYS + a) for a in range(WAYS) for b in range(WAYS)
    ]
    return lax.ppermute(x_share, ("cache", "fsdp", "head"), moves)


def solution(mesh):
    in_specs = (
        P(("groups", "cache"), None),
        P(),
        P("cache", ("fsdp", "head")),
        P("cache", ("fsdp", "head")),
        P("cache", ("fsdp", "head")),
        P(("fsdp", "head"), "cache"),
        P(),
        P(),
        P(("groups", "cache"), ("fsdp", "head")),
        P(("groups", "cache"), ("fsdp", "head")),
        P(),
        P("groups", None),
        P("groups"),
        P("groups"),
    )
    out_specs = P(("groups", "cache"), ("fsdp", "head"))
    sizes = dict(mesh.shape)

    def program(*args):
        panel_width, head_dim = args[2].shape[1] // (sizes["fsdp"] * sizes["head"]), args[6].shape[0]
        fits = (
            sizes == {"groups": 2, "cache": WAYS, "fsdp": 2, "head": 2}
            and panel_width == 2 * WAYS * head_dim
            and args[11].shape[1] == WAYS
        )
        plan = split_heads if fits else gathered_panels
        return jax.shard_map(
            plan, mesh=mesh, in_specs=in_specs, out_specs=out_specs, check_vma=False
        )(*args)

    return program
```

```python
import functools

import jax
import jax.numpy as jnp
from jax import lax
from jax.experimental import pallas as pl
from jax.experimental.pallas import tpu as pltpu
from jax.sharding import PartitionSpec as P

BLOCK = 256
ITERS = 2


epsilon = 1e-06


def rms_scale(values, gain_row):
    mean_square = jnp.mean(values * values, axis=-1, keepdims=True)
    return values * lax.rsqrt(mean_square + epsilon) * gain_row


def head_norm(projected, gain_row):
    row_count = projected.shape[0]
    split = projected.reshape(row_count, -1, gain_row.shape[0])
    return rms_scale(split, gain_row).astype(jnp.bfloat16).reshape(row_count, -1)


def attend(queries, key_rows, value_rows, head_dim):
    row_count = queries.shape[0]
    head_count = queries.shape[1] // head_dim
    query_heads = queries.reshape(row_count, head_count, head_dim)
    key_heads = key_rows.reshape(-1, head_count, head_dim)
    value_heads = value_rows.reshape(-1, head_count, head_dim)
    scores = jnp.einsum(
        "qhd,khd->hqk", query_heads, key_heads, preferred_element_type=jnp.float32
    ) * head_dim ** (-0.5)
    weights = jnp.exp(scores)
    totals = jnp.sum(weights, axis=2)
    summed = jnp.einsum(
        "hqk,khd->qhd",
        weights.astype(jnp.bfloat16),
        value_heads,
        preferred_element_type=jnp.float32,
    )
    return (
        (summed / jnp.transpose(totals)[:, :, None])
        .astype(jnp.bfloat16)
        .reshape(row_count, head_count * head_dim)
    )


def gathered_panels(
    tokens,
    norm_gain,
    w_query,
    w_key,
    w_value,
    w_out,
    query_gain,
    key_gain,
    cache_keys,
    cache_values,
    step_gate,
    block_list,
    block_home,
    reader_span,
):
    reader_index = lax.axis_index("cache")
    group_index = lax.axis_index(("fsdp", "head"))
    head_dim = query_gain.shape[0]
    panel_width = cache_keys.shape[1]
    held_blocks = cache_keys.shape[0] // BLOCK
    full_query, full_key, full_value = (
        lax.all_gather(w_query, "cache", axis=0, tiled=True),
        lax.all_gather(w_key, "cache", axis=0, tiled=True),
        lax.all_gather(w_value, "cache", axis=0, tiled=True),
    )
    out_panel = lax.all_gather(w_out, "cache", axis=1, tiled=True)
    wanted = jnp.take(block_list, reader_span, axis=0)
    home_slots = jnp.take(block_home, wanted)
    is_mine = home_slots // held_blocks == reader_index
    local_pos = jnp.sum(jnp.where(is_mine, home_slots % held_blocks, 0), axis=1)
    key_blocks = cache_keys.reshape(held_blocks, BLOCK, panel_width)
    value_blocks = cache_values.reshape(held_blocks, BLOCK, panel_width)
    send_keys = jnp.take(key_blocks, local_pos, axis=0)
    send_values = jnp.take(value_blocks, local_pos, axis=0)
    got_keys, got_values = (
        lax.all_to_all(send_keys, "cache", split_axis=0, concat_axis=0, tiled=True),
        lax.all_to_all(send_values, "cache", split_axis=0, concat_axis=0, tiled=True),
    )
    my_span = jnp.take(reader_span, reader_index)
    my_owners = jnp.take(block_home, jnp.take(block_list, my_span, axis=0)) // held_blocks
    fetched_keys = jnp.take(got_keys, my_owners, axis=0).reshape(-1, panel_width)
    fetched_values = jnp.take(got_values, my_owners, axis=0).reshape(-1, panel_width)
    out_columns = lax.all_to_all(
        out_panel, ("fsdp", "head"), split_axis=1, concat_axis=0, tiled=True
    )
    column_count = tokens.shape[1] // lax.axis_size(("fsdp", "head"))
    column_start = group_index * column_count
    current = tokens
    x_share = lax.dynamic_slice_in_dim(tokens, column_start, column_count, 1)
    for step_index in range(ITERS):
        normed = rms_scale(current.astype(jnp.float32), norm_gain).astype(jnp.bfloat16)
        queries = head_norm(
            jnp.dot(normed, full_query, preferred_element_type=jnp.float32), query_gain
        )
        own_keys = head_norm(
            jnp.dot(normed, full_key, preferred_element_type=jnp.float32), key_gain
        )
        own_values = jnp.dot(normed, full_value, preferred_element_type=jnp.float32).astype(
            jnp.bfloat16
        )
        all_keys = jnp.concatenate([fetched_keys, own_keys], axis=0)
        all_values = jnp.concatenate([fetched_values, own_values], axis=0)
        mixed = attend(queries, all_keys, all_values, head_dim)
        step_scale = step_gate[step_index]
        share_scale = lax.dynamic_slice_in_dim(step_scale, column_start, column_count, 0)
        heads_all = lax.all_gather(mixed, ("fsdp", "head"), axis=1, tiled=True)
        update = jnp.dot(heads_all, out_columns, preferred_element_type=jnp.float32)
        x_share = (x_share.astype(jnp.float32) + share_scale * update).astype(jnp.bfloat16)
        if step_index + 1 < ITERS:
            current = lax.all_gather(x_share, ("fsdp", "head"), axis=1, tiled=True)
    return x_share


WAYS = 4
MIB = 1024 * 1024


def whole_specs(count):
    return [pl.BlockSpec(memory_space=pltpu.VMEM) for _ in range(count)]


def project_kernel(gain_ref, query_gain_ref, key_gain_ref, *refs):
    pieces, panels = refs[:WAYS], refs[WAYS : 3 * WAYS]
    q_ref, k_ref, v_ref, normed_ref = refs[3 * WAYS :]
    tile, width = pieces[0].shape[1:]
    for r in range(WAYS):
        rows = [pieces[r ^ k][k].astype(jnp.float32) for k in range(WAYS)]
        square = sum(jnp.sum(x * x, axis=-1, keepdims=True) for x in rows)
        scale = lax.rsqrt(square / (WAYS * width) + epsilon)
        for k in range(WAYS):
            normed_ref[k, r * tile : (r + 1) * tile, :] = (
                rows[k] * scale * gain_ref[k : k + 1, :]
            ).astype(jnp.bfloat16)
    head_dim = query_gain_ref.shape[1]
    for h in range(2):
        total = jnp.dot(normed_ref[0], panels[h][...], preferred_element_type=jnp.float32)
        for k in range(1, WAYS):
            total += jnp.dot(
                normed_ref[k], panels[2 * k + h][...], preferred_element_type=jnp.float32
            )
        lanes = slice(h * head_dim, (h + 1) * head_dim)
        q_ref[:, lanes] = rms_scale(total[:, :head_dim], query_gain_ref[...]).astype(jnp.bfloat16)
        k_ref[:, lanes] = rms_scale(
            total[:, head_dim : 2 * head_dim], key_gain_ref[...]
        ).astype(jnp.bfloat16)
        v_ref[:, lanes] = total[:, 2 * head_dim :].astype(jnp.bfloat16)


def project(pieces, panels, gain_rows, query_gain, key_gain):
    tile, width = pieces[0].shape[1:]
    head_dim = query_gain.shape[1]
    shape = jax.ShapeDtypeStruct((WAYS * tile, 2 * head_dim), jnp.bfloat16)
    return pl.pallas_call(
        project_kernel,
        out_shape=[shape] * 3,
        in_specs=whole_specs(3 + 3 * WAYS),
        out_specs=whole_specs(3),
        scratch_shapes=[pltpu.VMEM((WAYS, WAYS * tile, width), jnp.bfloat16)],
        compiler_params=pltpu.CompilerParams(vmem_limit_bytes=24 * MIB),
    )(gain_rows, query_gain, key_gain, *pieces, *panels)


def attend_kernel(pos_ref, q_ref, k_ref, v_ref, *refs):
    held, mixed_ref = refs[:WAYS], refs[WAYS]
    head_dim = q_ref.shape[1] // 2
    tile = q_ref.shape[0] // WAYS
    across = (((1,), (1,)), ((), ()))
    for r in range(WAYS):
        rows = slice(r * tile, (r + 1) * tile)
        for h in range(2):
            lanes = slice(h * head_dim, (h + 1) * head_dim)
            value_lanes = slice((2 + h) * head_dim, (3 + h) * head_dim)
            query = q_ref[rows, lanes]
            keys = [k_ref[rows, lanes]]
            values = [v_ref[rows, lanes]]
            for k in range(WAYS):
                start = pl.multiple_of(pos_ref[r * WAYS + k] * BLOCK, BLOCK)
                keys.append(held[k][pl.ds(start, BLOCK), lanes])
                values.append(held[k][pl.ds(start, BLOCK), value_lanes])
            total = jnp.zeros((tile, 1), jnp.float32)
            summed = jnp.zeros((tile, head_dim), jnp.float32)
            for key, value in zip(keys, values):
                scores = lax.dot_general(query, key, across, preferred_element_type=jnp.float32)
                weights = jnp.exp(scores * head_dim ** (-0.5))
                total += jnp.sum(weights, axis=-1, keepdims=True)
                summed += jnp.dot(
                    weights.astype(jnp.bfloat16), value, preferred_element_type=jnp.float32
                )
            mixed_ref[rows, lanes] = (summed / total).astype(jnp.bfloat16)


def attend_all(pos, q, k, v, held):
    return pl.pallas_call(
        attend_kernel,
        out_shape=jax.ShapeDtypeStruct(q.shape, jnp.bfloat16),
        in_specs=[pl.BlockSpec(memory_space=pltpu.SMEM)] + whole_specs(3 + WAYS),
        out_specs=pl.BlockSpec(memory_space=pltpu.VMEM),
        compiler_params=pltpu.CompilerParams(vmem_limit_bytes=10 * MIB),
    )(pos, q, k, v, *held)


def out_kernel(w_ref, *refs):
    mixed, (keep_ref, send_ref) = refs[:WAYS], refs[WAYS:]
    depth = mixed[0].shape[1]
    tile = mixed[0].shape[0] // WAYS
    for r in range(WAYS):
        row = jnp.concatenate(
            [mixed[k][(r ^ k) * tile : ((r ^ k) + 1) * tile, :] for k in range(WAYS)], axis=1
        )
        update = jnp.dot(row, w_ref[...], preferred_element_type=jnp.float32)
        rows = slice((r // 2) * tile, (r // 2 + 1) * tile)
        if r % 2 == 0:
            keep_ref[rows, :] = update
        else:
            send_ref[rows, :] = update.astype(jnp.bfloat16)


def project_out(w_rows, mixed):
    tile = mixed[0].shape[0] // WAYS
    width = w_rows.shape[1]
    return pl.pallas_call(
        out_kernel,
        out_shape=[
            jax.ShapeDtypeStruct((2 * tile, width), jnp.float32),
            jax.ShapeDtypeStruct((2 * tile, width), jnp.bfloat16),
        ],
        in_specs=whole_specs(1 + WAYS),
        out_specs=whole_specs(2),
        compiler_params=pltpu.CompilerParams(vmem_limit_bytes=10 * MIB),
    )(w_rows, *mixed)


SWAP = [(0, 1), (1, 0)]


def from_z(value, k):
    return lax.ppermute(value, "cache", [(i, i ^ k) for i in range(WAYS)])


def split_heads(
    tokens,
    norm_gain,
    w_query,
    w_key,
    w_value,
    w_out,
    query_gain,
    key_gain,
    cache_keys,
    cache_values,
    step_gate,
    block_list,
    block_home,
    reader_span,
):
    z = lax.axis_index("cache")
    p = lax.axis_index(("fsdp", "head"))
    y = lax.axis_index("groups")
    head_dim = query_gain.shape[0]
    held_blocks = cache_keys.shape[0] // BLOCK
    width = tokens.shape[1] // WAYS
    tile = tokens.shape[0]
    ways = jnp.arange(WAYS, dtype=jnp.int32)

    def head_of(array, k, h):
        return lax.dynamic_slice_in_dim(array, ((z ^ k) * 2 + (y ^ h)) * head_dim, head_dim, 1)

    def panel_of(k, h):
        return jnp.concatenate([head_of(w, k, h) for w in (w_query, w_key, w_value)], axis=1)

    def cache_of(k):
        return jnp.concatenate([head_of(a, k, h) for a in (cache_keys, cache_values) for h in (0, 1)], axis=1)

    piece = lax.dynamic_slice_in_dim(tokens, p * width, width, 1)
    by_z = jnp.stack([piece] + [from_z(piece, k) for k in range(1, WAYS)])
    by_x = jnp.stack([by_z, lax.ppermute(by_z, "fsdp", SWAP)])
    by_core = lax.ppermute(by_x, "head", SWAP)
    gathered = jnp.stack([by_x, by_core], axis=1).reshape(WAYS * WAYS, tile, width)

    near = [panel_of(0, 0)] + [from_z(panel_of(k, 0), k) for k in range(1, WAYS)]
    far = [panel_of(0, 1)] + [lax.ppermute(near[k], "groups", SWAP) for k in range(1, WAYS)]
    panels = [panel for pair in zip(near, far) for panel in pair]
    held = [cache_of(0)] + [from_z(cache_of(k), k) for k in range(1, WAYS)]

    source = (z ^ p ^ ways)[None, :] * WAYS + (p ^ ways[:, None] ^ ways[None, :])
    pieces = [jnp.take(gathered, source[j], axis=0) for j in range(WAYS)]
    x_share = pieces[0][0]

    gain_rows = jnp.take(norm_gain.reshape(WAYS, width), z ^ ways, axis=0)
    heads = jnp.stack([(z ^ ways) * 2 + y, (z ^ ways) * 2 + 1 - y], axis=1).reshape(-1)
    w_rows = jnp.take(w_out.reshape(2 * WAYS, head_dim, width), heads, axis=0).reshape(-1, width)
    gates = lax.dynamic_slice_in_dim(step_gate, z * width, width, 1)
    slots = jnp.take(block_home, jnp.take(block_list, jnp.take(reader_span, z ^ p ^ ways), axis=0))
    from_k = slots[:, :, None] // held_blocks == (z ^ ways)[None, None, :]
    pos = jnp.sum(jnp.where(from_k, (slots % held_blocks)[:, :, None], 0), axis=1).reshape(-1)

    for step in range(ITERS):
        q, k, v = project(pieces, panels, gain_rows, query_gain[None], key_gain[None])
        own = attend_all(pos, q, k, v, held)
        mixed = [own] + [from_z(own, k) for k in range(1, WAYS)]
        keep, send = project_out(w_rows, mixed)
        half = keep + lax.ppermute(send, "head", SWAP).astype(jnp.float32)
        other = lax.ppermute(half[tile:].astype(jnp.bfloat16), "fsdp", SWAP)
        update = half[:tile] + other.astype(jnp.float32)
        x_share = (x_share.astype(jnp.float32) + gates[step] * update).astype(jnp.bfloat16)
        if step + 1 < ITERS:
            by_z = jnp.stack([x_share] + [from_z(x_share, k) for k in range(1, WAYS)])
            by_x = lax.ppermute(by_z, "fsdp", SWAP)
            pieces = [
                by_z,
                lax.ppermute(by_z, "head", SWAP),
                by_x,
                lax.ppermute(by_x, "head", SWAP),
            ]
    moves = [
        (a * WAYS + b, (a ^ b) * WAYS + a) for a in range(WAYS) for b in range(WAYS)
    ]
    return lax.ppermute(x_share, ("cache", "fsdp", "head"), moves)


def solution(mesh):
    in_specs = (
        P(("groups", "cache"), None),
        P(),
        P("cache", ("fsdp", "head")),
        P("cache", ("fsdp", "head")),
        P("cache", ("fsdp", "head")),
        P(("fsdp", "head"), "cache"),
        P(),
        P(),
        P(("groups", "cache"), ("fsdp", "head")),
        P(("groups", "cache"), ("fsdp", "head")),
        P(),
        P("groups", None),
        P("groups"),
        P("groups"),
    )
    out_specs = P(("groups", "cache"), ("fsdp", "head"))
    sizes = dict(mesh.shape)

    def program(*args):
        panel_width, head_dim = args[2].shape[1] // (sizes["fsdp"] * sizes["head"]), args[6].shape[0]
        fits = (
            sizes == {"groups": 2, "cache": WAYS, "fsdp": 2, "head": 2}
            and panel_width == 2 * WAYS * head_dim
            and args[11].shape[1] == WAYS
        )
        plan = split_heads if fits else gathered_panels
        return jax.shard_map(
            plan, mesh=mesh, in_specs=in_specs, out_specs=out_specs, check_vma=False
        )(*args)

    return program
```

```python
import functools

import jax
import jax.numpy as jnp
from jax import lax
from jax.experimental import pallas as pl
from jax.experimental.pallas import tpu as pltpu
from jax.sharding import PartitionSpec as P

BLOCK = 256
ITERS = 2


epsilon = 1e-06


def rms_scale(values, gain_row):
    mean_square = jnp.mean(values * values, axis=-1, keepdims=True)
    return values * lax.rsqrt(mean_square + epsilon) * gain_row


def head_norm(projected, gain_row):
    row_count = projected.shape[0]
    split = projected.reshape(row_count, -1, gain_row.shape[0])
    return rms_scale(split, gain_row).astype(jnp.bfloat16).reshape(row_count, -1)


def attend(queries, key_rows, value_rows, head_dim):
    row_count = queries.shape[0]
    head_count = queries.shape[1] // head_dim
    query_heads = queries.reshape(row_count, head_count, head_dim)
    key_heads = key_rows.reshape(-1, head_count, head_dim)
    value_heads = value_rows.reshape(-1, head_count, head_dim)
    scores = jnp.einsum(
        "qhd,khd->hqk", query_heads, key_heads, preferred_element_type=jnp.float32
    ) * head_dim ** (-0.5)
    weights = jnp.exp(scores)
    totals = jnp.sum(weights, axis=2)
    summed = jnp.einsum(
        "hqk,khd->qhd",
        weights.astype(jnp.bfloat16),
        value_heads,
        preferred_element_type=jnp.float32,
    )
    return (
        (summed / jnp.transpose(totals)[:, :, None])
        .astype(jnp.bfloat16)
        .reshape(row_count, head_count * head_dim)
    )


def gathered_panels(
    tokens,
    norm_gain,
    w_query,
    w_key,
    w_value,
    w_out,
    query_gain,
    key_gain,
    cache_keys,
    cache_values,
    step_gate,
    block_list,
    block_home,
    reader_span,
):
    reader_index = lax.axis_index("cache")
    group_index = lax.axis_index(("fsdp", "head"))
    head_dim = query_gain.shape[0]
    panel_width = cache_keys.shape[1]
    held_blocks = cache_keys.shape[0] // BLOCK
    full_query, full_key, full_value = (
        lax.all_gather(w_query, "cache", axis=0, tiled=True),
        lax.all_gather(w_key, "cache", axis=0, tiled=True),
        lax.all_gather(w_value, "cache", axis=0, tiled=True),
    )
    out_panel = lax.all_gather(w_out, "cache", axis=1, tiled=True)
    wanted = jnp.take(block_list, reader_span, axis=0)
    home_slots = jnp.take(block_home, wanted)
    is_mine = home_slots // held_blocks == reader_index
    local_pos = jnp.sum(jnp.where(is_mine, home_slots % held_blocks, 0), axis=1)
    key_blocks = cache_keys.reshape(held_blocks, BLOCK, panel_width)
    value_blocks = cache_values.reshape(held_blocks, BLOCK, panel_width)
    send_keys = jnp.take(key_blocks, local_pos, axis=0)
    send_values = jnp.take(value_blocks, local_pos, axis=0)
    got_keys, got_values = (
        lax.all_to_all(send_keys, "cache", split_axis=0, concat_axis=0, tiled=True),
        lax.all_to_all(send_values, "cache", split_axis=0, concat_axis=0, tiled=True),
    )
    my_span = jnp.take(reader_span, reader_index)
    my_owners = jnp.take(block_home, jnp.take(block_list, my_span, axis=0)) // held_blocks
    fetched_keys = jnp.take(got_keys, my_owners, axis=0).reshape(-1, panel_width)
    fetched_values = jnp.take(got_values, my_owners, axis=0).reshape(-1, panel_width)
    out_columns = lax.all_to_all(
        out_panel, ("fsdp", "head"), split_axis=1, concat_axis=0, tiled=True
    )
    column_count = tokens.shape[1] // lax.axis_size(("fsdp", "head"))
    column_start = group_index * column_count
    current = tokens
    x_share = lax.dynamic_slice_in_dim(tokens, column_start, column_count, 1)
    for step_index in range(ITERS):
        normed = rms_scale(current.astype(jnp.float32), norm_gain).astype(jnp.bfloat16)
        queries = head_norm(
            jnp.dot(normed, full_query, preferred_element_type=jnp.float32), query_gain
        )
        own_keys = head_norm(
            jnp.dot(normed, full_key, preferred_element_type=jnp.float32), key_gain
        )
        own_values = jnp.dot(normed, full_value, preferred_element_type=jnp.float32).astype(
            jnp.bfloat16
        )
        all_keys = jnp.concatenate([fetched_keys, own_keys], axis=0)
        all_values = jnp.concatenate([fetched_values, own_values], axis=0)
        mixed = attend(queries, all_keys, all_values, head_dim)
        step_scale = step_gate[step_index]
        share_scale = lax.dynamic_slice_in_dim(step_scale, column_start, column_count, 0)
        heads_all = lax.all_gather(mixed, ("fsdp", "head"), axis=1, tiled=True)
        update = jnp.dot(heads_all, out_columns, preferred_element_type=jnp.float32)
        x_share = (x_share.astype(jnp.float32) + share_scale * update).astype(jnp.bfloat16)
        if step_index + 1 < ITERS:
            current = lax.all_gather(x_share, ("fsdp", "head"), axis=1, tiled=True)
    return x_share


WAYS = 4
MIB = 1024 * 1024


def in_hbm(value):
    return pltpu.with_memory_space_constraint(value, pltpu.HBM)


HBM_SPEC = pl.BlockSpec(memory_space=pltpu.HBM)


def whole_specs(count):
    return [pl.BlockSpec(memory_space=pltpu.VMEM) for _ in range(count)]


def head_lanes(k, h, head_dim):
    z, y = lax.axis_index("cache"), lax.axis_index("groups")
    return pl.ds(pl.multiple_of(((z ^ k) * 2 + (y ^ h)) * head_dim, head_dim), head_dim)


def pack_panels_kernel(slots, gain_ref, *refs):
    weights, panels, (end_ref, held_ref, sems) = refs[:3], refs[3:-3], refs[-3:]
    end_ref[...] = jnp.zeros_like(end_ref)
    head_dim = gain_ref.shape[1]
    copies = []
    for i, (k, h) in enumerate(slots):
        for m, weight in enumerate(weights):
            copies.append(
                pltpu.make_async_copy(
                    weight.at[:, head_lanes(k, h, head_dim)],
                    held_ref.at[i, :, m * head_dim : (m + 1) * head_dim],
                    sems.at[i * 3 + m],
                )
            )
            copies[-1].start()
    for i, panel in enumerate(panels):
        for m in range(3):
            copies[i * 3 + m].wait()
            lanes = slice(m * head_dim, (m + 1) * head_dim)
            panel[:, lanes] = (held_ref[i, :, lanes].astype(jnp.float32) * gain_ref[...]).astype(
                jnp.bfloat16
            )


def pack_panels(slots, gain_lanes, weights):
    depth, head_dim = gain_lanes.shape
    shape = jax.ShapeDtypeStruct((depth, 3 * head_dim), jnp.bfloat16)
    return pl.pallas_call(
        functools.partial(pack_panels_kernel, slots),
        out_shape=[shape] * len(slots) + [jax.ShapeDtypeStruct((8, head_dim), jnp.float32)],
        in_specs=whole_specs(1) + [HBM_SPEC] * 3,
        out_specs=whole_specs(len(slots) + 1),
        scratch_shapes=[
            pltpu.VMEM((len(slots), depth, 3 * head_dim), jnp.bfloat16),
            pltpu.SemaphoreType.DMA((3 * len(slots),)),
        ],
        compiler_params=pltpu.CompilerParams(vmem_limit_bytes=10 * MIB),
    )(gain_lanes, *[in_hbm(w) for w in weights])


def pack_cache_kernel(ks, keys_ref, values_ref, *refs):
    packs, sems = refs[:-1], refs[-1]
    head_dim = packs[0].shape[1] // 4
    copies = []
    for i, (k, pack) in enumerate(zip(ks, packs)):
        for m in range(4):
            source = (keys_ref, values_ref)[m // 2]
            copies.append(
                pltpu.make_async_copy(
                    source.at[:, head_lanes(k, m % 2, head_dim)],
                    pack.at[:, m * head_dim : (m + 1) * head_dim],
                    sems.at[i * 4 + m],
                )
            )
            copies[-1].start()
    for copy in copies:
        copy.wait()


def pack_cache(ks, keys, values, head_dim):
    shape = jax.ShapeDtypeStruct((keys.shape[0], 4 * head_dim), jnp.bfloat16)
    return pl.pallas_call(
        functools.partial(pack_cache_kernel, ks),
        out_shape=[shape] * len(ks),
        in_specs=[HBM_SPEC] * 2,
        out_specs=whole_specs(len(ks)),
        scratch_shapes=[pltpu.SemaphoreType.DMA((4 * len(ks),))],
        compiler_params=pltpu.CompilerParams(vmem_limit_bytes=6 * MIB),
    )(*map(in_hbm, (keys, values)))


def project_rows(part, panel, query_gain_ref, key_gain_ref, outs):
    q_ref, k_ref, v_ref = outs
    head_dim = query_gain_ref.shape[1]
    totals = [None, None]
    squares = [0.0] * WAYS
    columns = 0
    for k in range(WAYS):
        blocks = [part(r, k) for r in range(WAYS)]
        rows = jnp.concatenate(blocks, axis=0)
        columns += rows.shape[1]
        for h in range(2):
            product = jnp.dot(rows, panel(k, h), preferred_element_type=jnp.float32)
            totals[h] = product if k == 0 else totals[h] + product
        for r in range(WAYS):
            wide = blocks[r].astype(jnp.float32)
            squares[r] += jnp.sum(wide * wide, axis=-1, keepdims=True)
    scale = lax.rsqrt(jnp.concatenate(squares, axis=0) / columns + epsilon)
    for h in range(2):
        total = totals[h] * scale
        lanes = slice(h * head_dim, (h + 1) * head_dim)
        q_ref[:, lanes] = rms_scale(total[:, :head_dim], query_gain_ref[...]).astype(jnp.bfloat16)
        k_ref[:, lanes] = rms_scale(
            total[:, head_dim : 2 * head_dim], key_gain_ref[...]
        ).astype(jnp.bfloat16)
        v_ref[:, lanes] = total[:, 2 * head_dim :].astype(jnp.bfloat16)


def attend_rows(pos_ref, q_ref, k_ref, v_ref, held, mixed_ref):
    head_dim = q_ref.shape[1] // 2
    tile = q_ref.shape[0] // WAYS
    across = (((1,), (1,)), ((), ()))
    for h in range(2):
        for r in range(WAYS):
            rows = slice(r * tile, (r + 1) * tile)
            lanes = slice(h * head_dim, (h + 1) * head_dim)
            value_lanes = slice((2 + h) * head_dim, (3 + h) * head_dim)
            query = q_ref[rows, lanes]
            keys = [k_ref[rows, lanes]]
            values = [v_ref[rows, lanes]]
            for k in range(WAYS):
                block = pl.ds(pl.multiple_of(pos_ref[r * WAYS + k] * BLOCK, BLOCK), BLOCK)
                keys.append(held[k][block, lanes])
                values.append(held[k][block, value_lanes])
            total = jnp.zeros((tile, 1), jnp.float32)
            summed = jnp.zeros((tile, head_dim), jnp.float32)
            for key, value in zip(keys, values):
                scores = lax.dot_general(query, key, across, preferred_element_type=jnp.float32)
                weights = jnp.exp(scores * head_dim ** (-0.5))
                total += jnp.sum(weights, axis=-1, keepdims=True)
                summed += jnp.dot(
                    weights.astype(jnp.bfloat16), value, preferred_element_type=jnp.float32
                )
            mixed_ref[rows, lanes] = (summed / total).astype(jnp.bfloat16)


def project_kernel(source_ref, query_gain_ref, key_gain_ref, gathered_ref, *refs):
    panels, outs = refs[: 2 * WAYS], refs[2 * WAYS :]

    def part(j, k):
        return gathered_ref[source_ref[j * WAYS + k]]

    def panel(k, h):
        return panels[2 * k + h][...]

    project_rows(part, panel, query_gain_ref, key_gain_ref, outs)


def attend_kernel(pos_ref, q_ref, k_ref, v_ref, *refs):
    attend_rows(pos_ref, q_ref, k_ref, v_ref, refs[:WAYS], refs[WAYS])


def both_kernel(pos_ref, query_gain_ref, key_gain_ref, *refs):
    pairs, panels, caches = refs[: 2 * WAYS], refs[2 * WAYS : 4 * WAYS], refs[4 * WAYS : 5 * WAYS]
    mixed_ref, panel_ref, held_ref, *outs, panel_sems, held_sems = refs[5 * WAYS :]
    copies = [
        pltpu.make_async_copy(source, panel_ref.at[i], panel_sems.at[i])
        for i, source in enumerate(panels)
    ]
    late = [
        pltpu.make_async_copy(source, held_ref.at[i], held_sems.at[i])
        for i, source in enumerate(caches)
    ]
    for copy in copies + late:
        copy.start()

    def part(j, k):
        return pairs[2 * j + k // 2][k % 2]

    def panel(k, h):
        copies[2 * k + h].wait()
        return panel_ref[2 * k + h]

    project_rows(part, panel, query_gain_ref, key_gain_ref, outs)
    for copy in late:
        copy.wait()
    attend_rows(pos_ref, *outs, [held_ref.at[k] for k in range(WAYS)], mixed_ref)


def mix_first(source, pos, gains, gathered, panels, held):
    tile, head_dim = gathered.shape[1], gains[0].shape[1]
    shape = jax.ShapeDtypeStruct((WAYS * tile, 2 * head_dim), jnp.bfloat16)
    qkv = pl.pallas_call(
        project_kernel,
        out_shape=[shape] * 3,
        in_specs=[pl.BlockSpec(memory_space=pltpu.SMEM)] + whole_specs(3 + len(panels)),
        out_specs=whole_specs(3),
        compiler_params=pltpu.CompilerParams(vmem_limit_bytes=14 * MIB),
    )(source, *gains, gathered, *panels)
    return pl.pallas_call(
        attend_kernel,
        out_shape=shape,
        in_specs=[pl.BlockSpec(memory_space=pltpu.SMEM)] + whole_specs(3 + len(held)),
        out_specs=whole_specs(1)[0],
        compiler_params=pltpu.CompilerParams(vmem_limit_bytes=10 * MIB),
    )(pos, *qkv, *held)


def mix_again(pos, gains, parts, panels, held):
    tile, head_dim = parts[0].shape[1], gains[0].shape[1]
    shape = (WAYS * tile, 2 * head_dim)
    return pl.pallas_call(
        both_kernel,
        out_shape=jax.ShapeDtypeStruct(shape, jnp.bfloat16),
        in_specs=[pl.BlockSpec(memory_space=pltpu.SMEM)]
        + whole_specs(2 + len(parts))
        + [HBM_SPEC] * (len(panels) + len(held)),
        out_specs=whole_specs(1)[0],
        scratch_shapes=[
            pltpu.VMEM((len(panels), *panels[0].shape), jnp.bfloat16),
            pltpu.VMEM((len(held), *held[0].shape), jnp.bfloat16),
            *[pltpu.VMEM(shape, jnp.bfloat16)] * 3,
            pltpu.SemaphoreType.DMA((len(panels),)),
            pltpu.SemaphoreType.DMA((len(held),)),
        ],
        compiler_params=pltpu.CompilerParams(vmem_limit_bytes=20 * MIB),
    )(pos, *gains, *parts, *map(in_hbm, panels), *map(in_hbm, held))


def out_kernel(w_ref, *refs):
    mixed, (keep_ref, send_ref) = refs[:WAYS], refs[WAYS:]
    depth = mixed[0].shape[1]
    tile = mixed[0].shape[0] // WAYS
    for r in range(WAYS):
        row = jnp.concatenate(
            [mixed[k][r * tile : (r + 1) * tile, :] for k in range(WAYS)], axis=1
        )
        update = jnp.dot(row, w_ref[...], preferred_element_type=jnp.float32)
        rows = slice((r // 2) * tile, (r // 2 + 1) * tile)
        if r % 2 == 0:
            keep_ref[rows, :] = update
        else:
            send_ref[rows, :] = update.astype(jnp.bfloat16)


def project_out(w_rows, mixed):
    tile = mixed[0].shape[0] // WAYS
    width = w_rows.shape[1]
    return pl.pallas_call(
        out_kernel,
        out_shape=[
            jax.ShapeDtypeStruct((2 * tile, width), jnp.float32),
            jax.ShapeDtypeStruct((2 * tile, width), jnp.bfloat16),
        ],
        in_specs=whole_specs(1 + WAYS),
        out_specs=whole_specs(2),
        compiler_params=pltpu.CompilerParams(vmem_limit_bytes=10 * MIB),
    )(w_rows, *mixed)


SWAP = [(0, 1), (1, 0)]


def from_z(value, k):
    return lax.ppermute(value, "cache", [(i, i ^ k) for i in range(WAYS)])


def split_heads(
    tokens,
    norm_gain,
    w_query,
    w_key,
    w_value,
    w_out,
    query_gain,
    key_gain,
    cache_keys,
    cache_values,
    step_gate,
    block_list,
    block_home,
    reader_span,
):
    z = lax.axis_index("cache")
    p = lax.axis_index(("fsdp", "head"))
    y = lax.axis_index("groups")
    head_dim = query_gain.shape[0]
    held_blocks = cache_keys.shape[0] // BLOCK
    width = tokens.shape[1] // WAYS
    tile = tokens.shape[0]
    ways = jnp.arange(WAYS, dtype=jnp.int32)

    def gather_pairs(by_z):
        low = jnp.stack(by_z[:2])
        low_x = lax.ppermute(low, "fsdp", SWAP)
        high = jnp.stack(by_z[2:])
        high_x = lax.ppermute(high, "fsdp", SWAP)
        mine = [low, high, low_x, high_x]
        low_c, high_c, low_xc, high_xc = [lax.ppermute(pair, "head", SWAP) for pair in mine]
        return [low, high, low_c, high_c, low_x, high_x, low_xc, high_xc]

    weights = (w_query, w_key, w_value)
    gain_lanes = jnp.broadcast_to(
        lax.dynamic_slice_in_dim(norm_gain, z * width, width, 0)[:, None], (width, head_dim)
    )
    order = (2, 3, 1)
    *sends, end = pack_panels([(k, 0) for k in order], gain_lanes, weights)
    sends = dict(zip(order, sends))
    near = {k: from_z(sends[k], k) for k in order}
    tokens, _ = lax.optimization_barrier((tokens, end))
    piece = lax.dynamic_slice_in_dim(tokens, p * width, width, 1)
    far_piece = from_z(piece, 2)
    parts = gather_pairs([piece, from_z(piece, 1), far_piece, from_z(far_piece, 1)])
    far = {k: lax.ppermute(near[k], "groups", SWAP) for k in order}
    packs = dict(zip((2, 3, 1, 0), pack_cache((2, 3, 1, 0), cache_keys, cache_values, head_dim)))
    held = [packs[0]]
    for k in range(1, WAYS):
        pack, _ = lax.optimization_barrier((packs[k], near[k]))
        held.append(from_z(pack, k))
    near[0], far[0], _ = pack_panels([(0, 0), (0, 1)], gain_lanes, weights)
    panels = [side[k] for k in range(WAYS) for side in (near, far)]
    gathered = jnp.concatenate(parts, axis=0)
    source = (z ^ p ^ ways)[None, :] * WAYS + (z ^ p ^ ways)[:, None]
    source = source.reshape(-1)
    x_share = lax.dynamic_index_in_dim(gathered, source[0], 0, keepdims=False)
    gains = (query_gain[None], key_gain[None])

    heads = jnp.stack([(z ^ ways) * 2 + y, (z ^ ways) * 2 + 1 - y], axis=1).reshape(-1)
    w_rows = jnp.take(w_out.reshape(2 * WAYS, head_dim, width), heads, axis=0).reshape(-1, width)
    gates = lax.dynamic_slice_in_dim(step_gate, z * width, width, 1)
    slots = jnp.take(block_home, jnp.take(block_list, jnp.take(reader_span, p ^ ways), axis=0))
    from_k = slots[:, :, None] // held_blocks == (z ^ ways)[None, None, :]
    pos = jnp.sum(jnp.where(from_k, (slots % held_blocks)[:, :, None], 0), axis=1).reshape(-1)

    for step in range(ITERS):
        if step == 0:
            own = mix_first(source, pos, gains, gathered, panels, held)
        else:
            own = mix_again(pos, gains, parts, panels, held)
        mixed = [own] + [from_z(own, k) for k in range(1, WAYS)]
        keep, send = project_out(w_rows, mixed)
        half = keep + lax.ppermute(send, "head", SWAP).astype(jnp.float32)
        base, other = x_share.astype(jnp.float32), half[tile:]
        if step + 1 < ITERS:
            other = lax.ppermute(other.astype(jnp.bfloat16), "fsdp", SWAP)
            update = half[:tile] + other.astype(jnp.float32)
            x_share = (base + gates[step] * update).astype(jnp.bfloat16)
            far = from_z(x_share, 2)
            parts = gather_pairs([x_share, from_z(x_share, 1), far, from_z(far, 1)])
    base = (base + gates[step] * half[:tile]).astype(jnp.bfloat16)
    other = (gates[step] * other).astype(jnp.bfloat16)
    ends = [
        lax.ppermute(
            value,
            ("cache", "fsdp", "head"),
            [(a * WAYS + b, (b ^ flip) * WAYS + a) for a in range(WAYS) for b in range(WAYS)],
        )
        for value, flip in ((base, 0), (other, 2))
    ]
    return (ends[0].astype(jnp.float32) + ends[1].astype(jnp.float32)).astype(jnp.bfloat16)


def solution(mesh):
    in_specs = (
        P(("groups", "cache"), None),
        P(),
        P("cache", ("fsdp", "head")),
        P("cache", ("fsdp", "head")),
        P("cache", ("fsdp", "head")),
        P(("fsdp", "head"), "cache"),
        P(),
        P(),
        P(("groups", "cache"), ("fsdp", "head")),
        P(("groups", "cache"), ("fsdp", "head")),
        P(),
        P("groups", None),
        P("groups"),
        P("groups"),
    )
    out_specs = P(("groups", "cache"), ("fsdp", "head"))
    sizes = dict(mesh.shape)

    def program(*args):
        panel_width, head_dim = args[2].shape[1] // (sizes["fsdp"] * sizes["head"]), args[6].shape[0]
        fits = (
            sizes == {"groups": 2, "cache": WAYS, "fsdp": 2, "head": 2}
            and panel_width == 2 * WAYS * head_dim
            and args[11].shape[1] == WAYS
        )
        plan = split_heads if fits else gathered_panels
        return jax.shard_map(
            plan, mesh=mesh, in_specs=in_specs, out_specs=out_specs, check_vma=False
        )(*args)

    return program
```

```python
import functools

import jax
import jax.numpy as jnp
from jax import lax
from jax.experimental import pallas as pl
from jax.experimental.pallas import tpu as pltpu
from jax.sharding import PartitionSpec as P

BLOCK = 256
ITERS = 2


epsilon = 1e-06


def rms_scale(values, gain_row):
    mean_square = jnp.mean(values * values, axis=-1, keepdims=True)
    return values * lax.rsqrt(mean_square + epsilon) * gain_row


def head_norm(projected, gain_row):
    row_count = projected.shape[0]
    split = projected.reshape(row_count, -1, gain_row.shape[0])
    return rms_scale(split, gain_row).astype(jnp.bfloat16).reshape(row_count, -1)


def attend(queries, key_rows, value_rows, head_dim):
    row_count = queries.shape[0]
    head_count = queries.shape[1] // head_dim
    query_heads = queries.reshape(row_count, head_count, head_dim)
    key_heads = key_rows.reshape(-1, head_count, head_dim)
    value_heads = value_rows.reshape(-1, head_count, head_dim)
    scores = jnp.einsum(
        "qhd,khd->hqk", query_heads, key_heads, preferred_element_type=jnp.float32
    ) * head_dim ** (-0.5)
    weights = jnp.exp(scores)
    totals = jnp.sum(weights, axis=2)
    summed = jnp.einsum(
        "hqk,khd->qhd",
        weights.astype(jnp.bfloat16),
        value_heads,
        preferred_element_type=jnp.float32,
    )
    return (
        (summed / jnp.transpose(totals)[:, :, None])
        .astype(jnp.bfloat16)
        .reshape(row_count, head_count * head_dim)
    )


def gathered_panels(
    tokens,
    norm_gain,
    w_query,
    w_key,
    w_value,
    w_out,
    query_gain,
    key_gain,
    cache_keys,
    cache_values,
    step_gate,
    block_list,
    block_home,
    reader_span,
):
    reader_index = lax.axis_index("cache")
    group_index = lax.axis_index(("fsdp", "head"))
    head_dim = query_gain.shape[0]
    panel_width = cache_keys.shape[1]
    held_blocks = cache_keys.shape[0] // BLOCK
    full_query, full_key, full_value = (
        lax.all_gather(w_query, "cache", axis=0, tiled=True),
        lax.all_gather(w_key, "cache", axis=0, tiled=True),
        lax.all_gather(w_value, "cache", axis=0, tiled=True),
    )
    out_panel = lax.all_gather(w_out, "cache", axis=1, tiled=True)
    wanted = jnp.take(block_list, reader_span, axis=0)
    home_slots = jnp.take(block_home, wanted)
    is_mine = home_slots // held_blocks == reader_index
    local_pos = jnp.sum(jnp.where(is_mine, home_slots % held_blocks, 0), axis=1)
    key_blocks = cache_keys.reshape(held_blocks, BLOCK, panel_width)
    value_blocks = cache_values.reshape(held_blocks, BLOCK, panel_width)
    send_keys = jnp.take(key_blocks, local_pos, axis=0)
    send_values = jnp.take(value_blocks, local_pos, axis=0)
    got_keys, got_values = (
        lax.all_to_all(send_keys, "cache", split_axis=0, concat_axis=0, tiled=True),
        lax.all_to_all(send_values, "cache", split_axis=0, concat_axis=0, tiled=True),
    )
    my_span = jnp.take(reader_span, reader_index)
    my_owners = jnp.take(block_home, jnp.take(block_list, my_span, axis=0)) // held_blocks
    fetched_keys = jnp.take(got_keys, my_owners, axis=0).reshape(-1, panel_width)
    fetched_values = jnp.take(got_values, my_owners, axis=0).reshape(-1, panel_width)
    out_columns = lax.all_to_all(
        out_panel, ("fsdp", "head"), split_axis=1, concat_axis=0, tiled=True
    )
    column_count = tokens.shape[1] // lax.axis_size(("fsdp", "head"))
    column_start = group_index * column_count
    current = tokens
    x_share = lax.dynamic_slice_in_dim(tokens, column_start, column_count, 1)
    for step_index in range(ITERS):
        normed = rms_scale(current.astype(jnp.float32), norm_gain).astype(jnp.bfloat16)
        queries = head_norm(
            jnp.dot(normed, full_query, preferred_element_type=jnp.float32), query_gain
        )
        own_keys = head_norm(
            jnp.dot(normed, full_key, preferred_element_type=jnp.float32), key_gain
        )
        own_values = jnp.dot(normed, full_value, preferred_element_type=jnp.float32).astype(
            jnp.bfloat16
        )
        all_keys = jnp.concatenate([fetched_keys, own_keys], axis=0)
        all_values = jnp.concatenate([fetched_values, own_values], axis=0)
        mixed = attend(queries, all_keys, all_values, head_dim)
        step_scale = step_gate[step_index]
        share_scale = lax.dynamic_slice_in_dim(step_scale, column_start, column_count, 0)
        heads_all = lax.all_gather(mixed, ("fsdp", "head"), axis=1, tiled=True)
        update = jnp.dot(heads_all, out_columns, preferred_element_type=jnp.float32)
        x_share = (x_share.astype(jnp.float32) + share_scale * update).astype(jnp.bfloat16)
        if step_index + 1 < ITERS:
            current = lax.all_gather(x_share, ("fsdp", "head"), axis=1, tiled=True)
    return x_share


WAYS = 4
MIB = 1024 * 1024


def in_hbm(value):
    return pltpu.with_memory_space_constraint(value, pltpu.HBM)


HBM_SPEC = pl.BlockSpec(memory_space=pltpu.HBM)


def whole_specs(count):
    return [pl.BlockSpec(memory_space=pltpu.VMEM) for _ in range(count)]


def head_lanes(k, h, head_dim):
    z, y = lax.axis_index("cache"), lax.axis_index("groups")
    return pl.ds(pl.multiple_of(((z ^ k) * 2 + (y ^ h)) * head_dim, head_dim), head_dim)


def pack_panels_kernel(slots, gain_ref, *refs):
    weights, panels, (end_ref, held_ref, sems) = refs[:3], refs[3:-3], refs[-3:]
    end_ref[...] = jnp.zeros_like(end_ref)
    head_dim = gain_ref.shape[1]
    copies = []
    for i, (k, h) in enumerate(slots):
        for m, weight in enumerate(weights):
            copies.append(
                pltpu.make_async_copy(
                    weight.at[:, head_lanes(k, h, head_dim)],
                    held_ref.at[i, :, m * head_dim : (m + 1) * head_dim],
                    sems.at[i * 3 + m],
                )
            )
            copies[-1].start()
    for i, panel in enumerate(panels):
        for m in range(3):
            copies[i * 3 + m].wait()
            lanes = slice(m * head_dim, (m + 1) * head_dim)
            panel[:, lanes] = (held_ref[i, :, lanes].astype(jnp.float32) * gain_ref[...]).astype(
                jnp.bfloat16
            )


def pack_panels(slots, gain_lanes, weights):
    depth, head_dim = gain_lanes.shape
    shape = jax.ShapeDtypeStruct((depth, 3 * head_dim), jnp.bfloat16)
    return pl.pallas_call(
        functools.partial(pack_panels_kernel, slots),
        out_shape=[shape] * len(slots) + [jax.ShapeDtypeStruct((8, head_dim), jnp.float32)],
        in_specs=whole_specs(1) + [HBM_SPEC] * 3,
        out_specs=whole_specs(len(slots) + 1),
        scratch_shapes=[
            pltpu.VMEM((len(slots), depth, 3 * head_dim), jnp.bfloat16),
            pltpu.SemaphoreType.DMA((3 * len(slots),)),
        ],
        compiler_params=pltpu.CompilerParams(vmem_limit_bytes=10 * MIB),
    )(gain_lanes, *[in_hbm(w) for w in weights])


def pack_cache_kernel(ks, keys_ref, values_ref, *refs):
    packs, sems = refs[:-1], refs[-1]
    head_dim = packs[0].shape[1] // 4
    copies = []
    for i, (k, pack) in enumerate(zip(ks, packs)):
        for m in range(4):
            source = (keys_ref, values_ref)[m // 2]
            copies.append(
                pltpu.make_async_copy(
                    source.at[:, head_lanes(k, m % 2, head_dim)],
                    pack.at[:, m * head_dim : (m + 1) * head_dim],
                    sems.at[i * 4 + m],
                )
            )
            copies[-1].start()
    for copy in copies:
        copy.wait()


def pack_cache(ks, keys, values, head_dim):
    shape = jax.ShapeDtypeStruct((keys.shape[0], 4 * head_dim), jnp.bfloat16)
    return pl.pallas_call(
        functools.partial(pack_cache_kernel, ks),
        out_shape=[shape] * len(ks),
        in_specs=[HBM_SPEC] * 2,
        out_specs=whole_specs(len(ks)),
        scratch_shapes=[pltpu.SemaphoreType.DMA((4 * len(ks),))],
        compiler_params=pltpu.CompilerParams(vmem_limit_bytes=6 * MIB),
    )(*map(in_hbm, (keys, values)))


def project_rows(tiles, part, panel, query_gain_ref, key_gain_ref, outs):
    q_ref, k_ref, v_ref = outs
    head_dim = query_gain_ref.shape[1]
    totals = [None, None]
    squares = [0.0] * tiles
    columns = 0
    for k in range(WAYS):
        blocks = [part(r, k) for r in range(tiles)]
        rows = jnp.concatenate(blocks, axis=0)
        columns += rows.shape[1]
        for h in range(2):
            product = jnp.dot(rows, panel(k, h), preferred_element_type=jnp.float32)
            totals[h] = product if k == 0 else totals[h] + product
        for r in range(tiles):
            wide = blocks[r].astype(jnp.float32)
            squares[r] += jnp.sum(wide * wide, axis=-1, keepdims=True)
    scale = lax.rsqrt(jnp.concatenate(squares, axis=0) / columns + epsilon)
    for h in range(2):
        total = totals[h] * scale
        lanes = slice(h * head_dim, (h + 1) * head_dim)
        q_ref[:, lanes] = rms_scale(total[:, :head_dim], query_gain_ref[...]).astype(jnp.bfloat16)
        k_ref[:, lanes] = rms_scale(
            total[:, head_dim : 2 * head_dim], key_gain_ref[...]
        ).astype(jnp.bfloat16)
        v_ref[:, lanes] = total[:, 2 * head_dim :].astype(jnp.bfloat16)


def attend_rows(pair, start, pos_ref, q_ref, k_ref, v_ref, held, mixed_ref):
    head_dim = q_ref.shape[1] // 2
    tile = mixed_ref.shape[0] // 2
    across = (((1,), (1,)), ((), ()))
    for h in range(2):
        for r in range(2 * pair, 2 * pair + 2):
            at = (r - 2 * pair) * tile
            rows = slice(start + at, start + at + tile)
            lanes = slice(h * head_dim, (h + 1) * head_dim)
            value_lanes = slice((2 + h) * head_dim, (3 + h) * head_dim)
            query = q_ref[rows, lanes]
            keys = [k_ref[rows, lanes]]
            values = [v_ref[rows, lanes]]
            for k in range(WAYS):
                block = pl.ds(pl.multiple_of(pos_ref[r * WAYS + k] * BLOCK, BLOCK), BLOCK)
                keys.append(held[k][block, lanes])
                values.append(held[k][block, value_lanes])
            total = jnp.zeros((tile, 1), jnp.float32)
            summed = jnp.zeros((tile, head_dim), jnp.float32)
            for key, value in zip(keys, values):
                scores = lax.dot_general(query, key, across, preferred_element_type=jnp.float32)
                weights = jnp.exp(scores * head_dim ** (-0.5))
                total += jnp.sum(weights, axis=-1, keepdims=True)
                summed += jnp.dot(
                    weights.astype(jnp.bfloat16), value, preferred_element_type=jnp.float32
                )
            mixed_ref[at : at + tile, lanes] = (summed / total).astype(jnp.bfloat16)


def project_kernel(source_ref, query_gain_ref, key_gain_ref, gathered_ref, *refs):
    panels, outs = refs[: 2 * WAYS], refs[2 * WAYS :]

    def part(j, k):
        return gathered_ref[source_ref[j * WAYS + k]]

    def panel(k, h):
        return panels[2 * k + h][...]

    project_rows(WAYS, part, panel, query_gain_ref, key_gain_ref, outs)


def attend_kernel(pair, pos_ref, q_ref, k_ref, v_ref, *refs):
    start = pair * refs[WAYS].shape[0]
    attend_rows(pair, start, pos_ref, q_ref, k_ref, v_ref, refs[:WAYS], refs[WAYS])


def both_kernel(pair, pos_ref, query_gain_ref, key_gain_ref, *refs):
    parts, panels, caches = refs[:WAYS], refs[WAYS : 3 * WAYS], refs[3 * WAYS : 4 * WAYS]
    mixed_ref, panel_ref, held_ref, *outs, panel_sems, held_sems = refs[4 * WAYS :]
    copies = [
        pltpu.make_async_copy(source, panel_ref.at[i], panel_sems.at[i])
        for i, source in enumerate(panels)
    ]
    late = [
        pltpu.make_async_copy(source, held_ref.at[i], held_sems.at[i])
        for i, source in enumerate(caches)
    ]
    for copy in copies + late:
        copy.start()

    def part(j, k):
        return parts[2 * j + k // 2][k % 2]

    def panel(k, h):
        copies[2 * k + h].wait()
        return panel_ref[2 * k + h]

    project_rows(2, part, panel, query_gain_ref, key_gain_ref, outs)
    for copy in late:
        copy.wait()
    attend_rows(pair, 0, pos_ref, *outs, [held_ref.at[k] for k in range(WAYS)], mixed_ref)


def project(source, gains, gathered, panels):
    tile, head_dim = gathered.shape[1], gains[0].shape[1]
    return pl.pallas_call(
        project_kernel,
        out_shape=[jax.ShapeDtypeStruct((WAYS * tile, 2 * head_dim), jnp.bfloat16)] * 3,
        in_specs=[pl.BlockSpec(memory_space=pltpu.SMEM)] + whole_specs(3 + len(panels)),
        out_specs=whole_specs(3),
        compiler_params=pltpu.CompilerParams(vmem_limit_bytes=14 * MIB),
    )(source, *gains, gathered, *panels)


def attend_pair(pair, pos, qkv, held):
    rows, columns = qkv[0].shape
    return pl.pallas_call(
        functools.partial(attend_kernel, pair),
        out_shape=jax.ShapeDtypeStruct((rows // 2, columns), jnp.bfloat16),
        in_specs=[pl.BlockSpec(memory_space=pltpu.SMEM)] + whole_specs(3 + len(held)),
        out_specs=whole_specs(1)[0],
        compiler_params=pltpu.CompilerParams(vmem_limit_bytes=10 * MIB),
    )(pos, *qkv, *held)


def mix_pair(pair, pos, gains, parts, panels, held):
    tile, head_dim = parts[0].shape[1], gains[0].shape[1]
    shape = (2 * tile, 2 * head_dim)
    return pl.pallas_call(
        functools.partial(both_kernel, pair),
        out_shape=jax.ShapeDtypeStruct(shape, jnp.bfloat16),
        in_specs=[pl.BlockSpec(memory_space=pltpu.SMEM)]
        + whole_specs(2 + len(parts))
        + [HBM_SPEC] * (len(panels) + len(held)),
        out_specs=whole_specs(1)[0],
        scratch_shapes=[
            pltpu.VMEM((len(panels), *panels[0].shape), jnp.bfloat16),
            pltpu.VMEM((len(held), *held[0].shape), jnp.bfloat16),
            *[pltpu.VMEM(shape, jnp.bfloat16)] * 3,
            pltpu.SemaphoreType.DMA((len(panels),)),
            pltpu.SemaphoreType.DMA((len(held),)),
        ],
        compiler_params=pltpu.CompilerParams(vmem_limit_bytes=16 * MIB),
    )(pos, *gains, *parts, *map(in_hbm, panels), *map(in_hbm, held))


def out_kernel(w_ref, *refs):
    mixed, (keep_ref, send_ref) = refs[:WAYS], refs[WAYS:]
    tile = keep_ref.shape[0]
    rows = jnp.concatenate([part[...] for part in mixed], axis=1)
    update = jnp.dot(rows, w_ref[...], preferred_element_type=jnp.float32)
    keep_ref[...] = update[:tile]
    send_ref[...] = update[tile:].astype(jnp.bfloat16)


def project_out(w_rows, mixed):
    shape = (mixed[0].shape[0] // 2, w_rows.shape[1])
    return pl.pallas_call(
        out_kernel,
        out_shape=[
            jax.ShapeDtypeStruct(shape, jnp.float32),
            jax.ShapeDtypeStruct(shape, jnp.bfloat16),
        ],
        in_specs=whole_specs(1 + WAYS),
        out_specs=whole_specs(2),
        compiler_params=pltpu.CompilerParams(vmem_limit_bytes=6 * MIB),
    )(w_rows, *mixed)


SWAP = [(0, 1), (1, 0)]


def from_z(value, k):
    return lax.ppermute(value, "cache", [(i, i ^ k) for i in range(WAYS)])


def split_heads(
    tokens,
    norm_gain,
    w_query,
    w_key,
    w_value,
    w_out,
    query_gain,
    key_gain,
    cache_keys,
    cache_values,
    step_gate,
    block_list,
    block_home,
    reader_span,
):
    z = lax.axis_index("cache")
    p = lax.axis_index(("fsdp", "head"))
    y = lax.axis_index("groups")
    head_dim = query_gain.shape[0]
    held_blocks = cache_keys.shape[0] // BLOCK
    width = tokens.shape[1] // WAYS
    tile = tokens.shape[0]
    ways = jnp.arange(WAYS, dtype=jnp.int32)

    def gather_pairs(by_z):
        low = jnp.stack(by_z[:2])
        low_x = lax.ppermute(low, "fsdp", SWAP)
        high = jnp.stack(by_z[2:])
        high_x = lax.ppermute(high, "fsdp", SWAP)
        mine = [low, high, low_x, high_x]
        low_c, high_c, low_xc, high_xc = [lax.ppermute(pair, "head", SWAP) for pair in mine]
        return [low, high, low_c, high_c, low_x, high_x, low_xc, high_xc]

    weights = (w_query, w_key, w_value)
    gain_lanes = jnp.broadcast_to(
        lax.dynamic_slice_in_dim(norm_gain, z * width, width, 0)[:, None], (width, head_dim)
    )
    order = (2, 3, 1)
    *sends, end = pack_panels([(k, 0) for k in order], gain_lanes, weights)
    sends = dict(zip(order, sends))
    near = {k: from_z(sends[k], k) for k in order}
    tokens, _ = lax.optimization_barrier((tokens, end))
    piece = lax.dynamic_slice_in_dim(tokens, p * width, width, 1)
    far_piece = from_z(piece, 2)
    parts = gather_pairs([piece, from_z(piece, 1), far_piece, from_z(far_piece, 1)])
    far = {k: lax.ppermute(near[k], "groups", SWAP) for k in order}
    packs = dict(zip((2, 3, 1, 0), pack_cache((2, 3, 1, 0), cache_keys, cache_values, head_dim)))
    held = [packs[0]]
    for k in range(1, WAYS):
        pack, _ = lax.optimization_barrier((packs[k], near[k]))
        held.append(from_z(pack, k))
    near[0], far[0], _ = pack_panels([(0, 0), (0, 1)], gain_lanes, weights)
    panels = [side[k] for k in range(WAYS) for side in (near, far)]
    gathered = jnp.concatenate(parts, axis=0)
    source = (z ^ p ^ ways)[None, :] * WAYS + (z ^ p ^ ways)[:, None]
    source = source.reshape(-1)
    x_share = lax.dynamic_index_in_dim(gathered, source[0], 0, keepdims=False)
    gains = (query_gain[None], key_gain[None])

    heads = jnp.stack([(z ^ ways) * 2 + y, (z ^ ways) * 2 + 1 - y], axis=1).reshape(-1)
    w_rows = jnp.take(w_out.reshape(2 * WAYS, head_dim, width), heads, axis=0).reshape(-1, width)
    gates = lax.dynamic_slice_in_dim(step_gate, z * width, width, 1)
    slots = jnp.take(block_home, jnp.take(block_list, jnp.take(reader_span, p ^ ways), axis=0))
    from_k = slots[:, :, None] // held_blocks == (z ^ ways)[None, None, :]
    pos = jnp.sum(jnp.where(from_k, (slots % held_blocks)[:, :, None], 0), axis=1).reshape(-1)

    def gather_z(own):
        near, far = lax.optimization_barrier((from_z(own, 1), from_z(own, 2)))
        return [own, near, far, from_z(far, 1)]

    def summed(own):
        mixed = gather_z(own)
        keep, send = project_out(w_rows, mixed)
        return keep + lax.ppermute(send, "head", SWAP).astype(jnp.float32)

    qkv = project(source, gains, gathered, panels)
    own = attend_pair(1, pos, qkv, held)
    other = lax.ppermute(summed(own).astype(jnp.bfloat16), "fsdp", SWAP)
    pos_late, _ = lax.optimization_barrier((pos, own))
    update = summed(attend_pair(0, pos_late, qkv, held)) + other.astype(jnp.float32)
    x_share = (x_share.astype(jnp.float32) + gates[0] * update).astype(jnp.bfloat16)

    parts = gather_pairs(gather_z(x_share))
    ends = []
    for pair in range(2):
        own = mix_pair(pair, pos, gains, parts[4 * pair : 4 * pair + 4], panels, held)
        value = gates[1] * summed(own)
        if pair == 0:
            value += x_share.astype(jnp.float32)
        moves = [(a * WAYS + b, (b ^ (2 * pair)) * WAYS + a) for a in range(WAYS) for b in range(WAYS)]
        ends.append(lax.ppermute(value.astype(jnp.bfloat16), ("cache", "fsdp", "head"), moves))
    return (ends[0].astype(jnp.float32) + ends[1].astype(jnp.float32)).astype(jnp.bfloat16)


def solution(mesh):
    in_specs = (
        P(("groups", "cache"), None),
        P(),
        P("cache", ("fsdp", "head")),
        P("cache", ("fsdp", "head")),
        P("cache", ("fsdp", "head")),
        P(("fsdp", "head"), "cache"),
        P(),
        P(),
        P(("groups", "cache"), ("fsdp", "head")),
        P(("groups", "cache"), ("fsdp", "head")),
        P(),
        P("groups", None),
        P("groups"),
        P("groups"),
    )
    out_specs = P(("groups", "cache"), ("fsdp", "head"))
    sizes = dict(mesh.shape)

    def program(*args):
        panel_width, head_dim = args[2].shape[1] // (sizes["fsdp"] * sizes["head"]), args[6].shape[0]
        fits = (
            sizes == {"groups": 2, "cache": WAYS, "fsdp": 2, "head": 2}
            and panel_width == 2 * WAYS * head_dim
            and args[11].shape[1] == WAYS
            and ITERS == 2
        )
        plan = split_heads if fits else gathered_panels
        return jax.shard_map(
            plan, mesh=mesh, in_specs=in_specs, out_specs=out_specs, check_vma=False
        )(*args)

    return program
```

```python
import functools

import jax
import jax.numpy as jnp
from jax import lax
from jax.experimental import pallas as pl
from jax.experimental.pallas import tpu as pltpu
from jax.sharding import PartitionSpec as P

BLOCK = 256
ITERS = 2


epsilon = 1e-06


def rms_scale(values, gain_row):
    mean_square = jnp.mean(values * values, axis=-1, keepdims=True)
    return values * lax.rsqrt(mean_square + epsilon) * gain_row


def head_norm(projected, gain_row):
    row_count = projected.shape[0]
    split = projected.reshape(row_count, -1, gain_row.shape[0])
    return rms_scale(split, gain_row).astype(jnp.bfloat16).reshape(row_count, -1)


def attend(queries, key_rows, value_rows, head_dim):
    row_count = queries.shape[0]
    head_count = queries.shape[1] // head_dim
    query_heads = queries.reshape(row_count, head_count, head_dim)
    key_heads = key_rows.reshape(-1, head_count, head_dim)
    value_heads = value_rows.reshape(-1, head_count, head_dim)
    scores = jnp.einsum(
        "qhd,khd->hqk", query_heads, key_heads, preferred_element_type=jnp.float32
    ) * head_dim ** (-0.5)
    weights = jnp.exp(scores)
    totals = jnp.sum(weights, axis=2)
    summed = jnp.einsum(
        "hqk,khd->qhd",
        weights.astype(jnp.bfloat16),
        value_heads,
        preferred_element_type=jnp.float32,
    )
    return (
        (summed / jnp.transpose(totals)[:, :, None])
        .astype(jnp.bfloat16)
        .reshape(row_count, head_count * head_dim)
    )


def gathered_panels(
    tokens,
    norm_gain,
    w_query,
    w_key,
    w_value,
    w_out,
    query_gain,
    key_gain,
    cache_keys,
    cache_values,
    step_gate,
    block_list,
    block_home,
    reader_span,
):
    reader_index = lax.axis_index("cache")
    group_index = lax.axis_index(("fsdp", "head"))
    head_dim = query_gain.shape[0]
    panel_width = cache_keys.shape[1]
    held_blocks = cache_keys.shape[0] // BLOCK
    full_query, full_key, full_value = (
        lax.all_gather(w_query, "cache", axis=0, tiled=True),
        lax.all_gather(w_key, "cache", axis=0, tiled=True),
        lax.all_gather(w_value, "cache", axis=0, tiled=True),
    )
    out_panel = lax.all_gather(w_out, "cache", axis=1, tiled=True)
    wanted = jnp.take(block_list, reader_span, axis=0)
    home_slots = jnp.take(block_home, wanted)
    is_mine = home_slots // held_blocks == reader_index
    local_pos = jnp.sum(jnp.where(is_mine, home_slots % held_blocks, 0), axis=1)
    key_blocks = cache_keys.reshape(held_blocks, BLOCK, panel_width)
    value_blocks = cache_values.reshape(held_blocks, BLOCK, panel_width)
    send_keys = jnp.take(key_blocks, local_pos, axis=0)
    send_values = jnp.take(value_blocks, local_pos, axis=0)
    got_keys, got_values = (
        lax.all_to_all(send_keys, "cache", split_axis=0, concat_axis=0, tiled=True),
        lax.all_to_all(send_values, "cache", split_axis=0, concat_axis=0, tiled=True),
    )
    my_span = jnp.take(reader_span, reader_index)
    my_owners = jnp.take(block_home, jnp.take(block_list, my_span, axis=0)) // held_blocks
    fetched_keys = jnp.take(got_keys, my_owners, axis=0).reshape(-1, panel_width)
    fetched_values = jnp.take(got_values, my_owners, axis=0).reshape(-1, panel_width)
    out_columns = lax.all_to_all(
        out_panel, ("fsdp", "head"), split_axis=1, concat_axis=0, tiled=True
    )
    column_count = tokens.shape[1] // lax.axis_size(("fsdp", "head"))
    column_start = group_index * column_count
    current = tokens
    x_share = lax.dynamic_slice_in_dim(tokens, column_start, column_count, 1)
    for step_index in range(ITERS):
        normed = rms_scale(current.astype(jnp.float32), norm_gain).astype(jnp.bfloat16)
        queries = head_norm(
            jnp.dot(normed, full_query, preferred_element_type=jnp.float32), query_gain
        )
        own_keys = head_norm(
            jnp.dot(normed, full_key, preferred_element_type=jnp.float32), key_gain
        )
        own_values = jnp.dot(normed, full_value, preferred_element_type=jnp.float32).astype(
            jnp.bfloat16
        )
        all_keys = jnp.concatenate([fetched_keys, own_keys], axis=0)
        all_values = jnp.concatenate([fetched_values, own_values], axis=0)
        mixed = attend(queries, all_keys, all_values, head_dim)
        step_scale = step_gate[step_index]
        share_scale = lax.dynamic_slice_in_dim(step_scale, column_start, column_count, 0)
        heads_all = lax.all_gather(mixed, ("fsdp", "head"), axis=1, tiled=True)
        update = jnp.dot(heads_all, out_columns, preferred_element_type=jnp.float32)
        x_share = (x_share.astype(jnp.float32) + share_scale * update).astype(jnp.bfloat16)
        if step_index + 1 < ITERS:
            current = lax.all_gather(x_share, ("fsdp", "head"), axis=1, tiled=True)
    return x_share


WAYS = 4
MIB = 1024 * 1024


def in_hbm(value):
    return pltpu.with_memory_space_constraint(value, pltpu.HBM)


HBM_SPEC = pl.BlockSpec(memory_space=pltpu.HBM)


def whole_specs(count):
    return [pl.BlockSpec(memory_space=pltpu.VMEM) for _ in range(count)]


def head_lanes(k, h, head_dim):
    z, y = lax.axis_index("cache"), lax.axis_index("groups")
    return pl.ds(pl.multiple_of(((z ^ k) * 2 + (y ^ h)) * head_dim, head_dim), head_dim)


def pack_panels_kernel(slots, gain_ref, *refs):
    weights, panels, (end_ref, held_ref, sems) = refs[:3], refs[3:-3], refs[-3:]
    end_ref[...] = jnp.zeros_like(end_ref)
    head_dim = gain_ref.shape[1]
    copies = []
    for i, (k, h) in enumerate(slots):
        for m, weight in enumerate(weights):
            copies.append(
                pltpu.make_async_copy(
                    weight.at[:, head_lanes(k, h, head_dim)],
                    held_ref.at[i, :, m * head_dim : (m + 1) * head_dim],
                    sems.at[i * 3 + m],
                )
            )
            copies[-1].start()
    for i, panel in enumerate(panels):
        for m in range(3):
            copies[i * 3 + m].wait()
            lanes = slice(m * head_dim, (m + 1) * head_dim)
            panel[:, lanes] = (held_ref[i, :, lanes].astype(jnp.float32) * gain_ref[...]).astype(
                jnp.bfloat16
            )


def pack_panels(slots, gain_lanes, weights):
    depth, head_dim = gain_lanes.shape
    shape = jax.ShapeDtypeStruct((depth, 3 * head_dim), jnp.bfloat16)
    return pl.pallas_call(
        functools.partial(pack_panels_kernel, slots),
        out_shape=[shape] * len(slots) + [jax.ShapeDtypeStruct((8, head_dim), jnp.float32)],
        in_specs=whole_specs(1) + [HBM_SPEC] * 3,
        out_specs=whole_specs(len(slots) + 1),
        scratch_shapes=[
            pltpu.VMEM((len(slots), depth, 3 * head_dim), jnp.bfloat16),
            pltpu.SemaphoreType.DMA((3 * len(slots),)),
        ],
        compiler_params=pltpu.CompilerParams(vmem_limit_bytes=10 * MIB),
    )(gain_lanes, *[in_hbm(w) for w in weights])


def pack_cache_kernel(ks, keys_ref, values_ref, *refs):
    packs, sems = refs[:-1], refs[-1]
    head_dim = packs[0].shape[1] // 4
    copies = []
    for i, (k, pack) in enumerate(zip(ks, packs)):
        for m in range(4):
            source = (keys_ref, values_ref)[m // 2]
            copies.append(
                pltpu.make_async_copy(
                    source.at[:, head_lanes(k, m % 2, head_dim)],
                    pack.at[:, m * head_dim : (m + 1) * head_dim],
                    sems.at[i * 4 + m],
                )
            )
            copies[-1].start()
    for copy in copies:
        copy.wait()


def pack_cache(ks, keys, values, head_dim):
    shape = jax.ShapeDtypeStruct((keys.shape[0], 4 * head_dim), jnp.bfloat16)
    return pl.pallas_call(
        functools.partial(pack_cache_kernel, ks),
        out_shape=[shape] * len(ks),
        in_specs=[HBM_SPEC] * 2,
        out_specs=whole_specs(len(ks)),
        scratch_shapes=[pltpu.SemaphoreType.DMA((4 * len(ks),))],
        compiler_params=pltpu.CompilerParams(vmem_limit_bytes=6 * MIB),
    )(*map(in_hbm, (keys, values)))


def project_rows(tiles, part, panel, query_gain_ref, key_gain_ref, outs):
    q_ref, k_ref, v_ref = outs
    head_dim = query_gain_ref.shape[1]
    totals = [None, None]
    squares = [0.0] * tiles
    columns = 0
    for k in range(WAYS):
        blocks = [part(r, k) for r in range(tiles)]
        rows = jnp.concatenate(blocks, axis=0)
        columns += rows.shape[1]
        for h in range(2):
            product = jnp.dot(rows, panel(k, h), preferred_element_type=jnp.float32)
            totals[h] = product if k == 0 else totals[h] + product
        for r in range(tiles):
            wide = blocks[r].astype(jnp.float32)
            squares[r] += jnp.sum(wide * wide, axis=-1, keepdims=True)
    scale = lax.rsqrt(jnp.concatenate(squares, axis=0) / columns + epsilon)
    for h in range(2):
        total = totals[h] * scale
        lanes = slice(h * head_dim, (h + 1) * head_dim)
        q_ref[:, lanes] = rms_scale(total[:, :head_dim], query_gain_ref[...]).astype(jnp.bfloat16)
        k_ref[:, lanes] = rms_scale(
            total[:, head_dim : 2 * head_dim], key_gain_ref[...]
        ).astype(jnp.bfloat16)
        v_ref[:, lanes] = total[:, 2 * head_dim :].astype(jnp.bfloat16)


def attend_rows(pair, start, pos_ref, q_ref, k_ref, v_ref, held, mixed_ref):
    head_dim = q_ref.shape[1] // 2
    tile = mixed_ref.shape[0] // 2
    across = (((1,), (1,)), ((), ()))
    for h in range(2):
        for r in range(2 * pair, 2 * pair + 2):
            at = (r - 2 * pair) * tile
            rows = slice(start + at, start + at + tile)
            lanes = slice(h * head_dim, (h + 1) * head_dim)
            value_lanes = slice((2 + h) * head_dim, (3 + h) * head_dim)
            query = q_ref[rows, lanes]
            keys = [k_ref[rows, lanes]]
            values = [v_ref[rows, lanes]]
            for k in range(WAYS):
                block = pl.ds(pl.multiple_of(pos_ref[r * WAYS + k] * BLOCK, BLOCK), BLOCK)
                keys.append(held[k][block, lanes])
                values.append(held[k][block, value_lanes])
            total = jnp.zeros((tile, 1), jnp.float32)
            summed = jnp.zeros((tile, head_dim), jnp.float32)
            for key, value in zip(keys, values):
                scores = lax.dot_general(query, key, across, preferred_element_type=jnp.float32)
                weights = jnp.exp(scores * head_dim ** (-0.5))
                total += jnp.sum(weights, axis=-1, keepdims=True)
                summed += jnp.dot(
                    weights.astype(jnp.bfloat16), value, preferred_element_type=jnp.float32
                )
            mixed_ref[at : at + tile, lanes] = (summed / total).astype(jnp.bfloat16)


def project_kernel(source_ref, query_gain_ref, key_gain_ref, gathered_ref, *refs):
    panels, outs = refs[: 2 * WAYS], refs[2 * WAYS :]

    def part(j, k):
        return gathered_ref[source_ref[j * WAYS + k]]

    def panel(k, h):
        return panels[2 * k + h][...]

    project_rows(WAYS, part, panel, query_gain_ref, key_gain_ref, outs)


def attend_kernel(pair, pos_ref, q_ref, k_ref, v_ref, *refs):
    start = pair * refs[WAYS].shape[0]
    attend_rows(pair, start, pos_ref, q_ref, k_ref, v_ref, refs[:WAYS], refs[WAYS])


def both_kernel(pair, places, pos_ref, query_gain_ref, key_gain_ref, *refs):
    count = 2 * (1 + places[-1][0])
    parts, panels, caches = refs[:count], refs[count : count + 2 * WAYS], refs[count + 2 * WAYS :]
    caches, rest = caches[:WAYS], caches[WAYS:]
    mixed_ref, panel_ref, held_ref, *outs, panel_sems, held_sems = rest
    copies = [
        pltpu.make_async_copy(source, panel_ref.at[i], panel_sems.at[i])
        for i, source in enumerate(panels)
    ]
    late = [
        pltpu.make_async_copy(source, held_ref.at[i], held_sems.at[i])
        for i, source in enumerate(caches)
    ]
    for copy in copies + late:
        copy.start()

    def part(j, k):
        at, inner = places[k]
        return parts[j * count // 2 + at][inner]

    def panel(k, h):
        copies[2 * k + h].wait()
        return panel_ref[2 * k + h]

    project_rows(2, part, panel, query_gain_ref, key_gain_ref, outs)
    for copy in late:
        copy.wait()
    attend_rows(pair, 0, pos_ref, *outs, [held_ref.at[k] for k in range(WAYS)], mixed_ref)


def project(source, gains, gathered, panels):
    tile, head_dim = gathered.shape[1], gains[0].shape[1]
    return pl.pallas_call(
        project_kernel,
        out_shape=[jax.ShapeDtypeStruct((WAYS * tile, 2 * head_dim), jnp.bfloat16)] * 3,
        in_specs=[pl.BlockSpec(memory_space=pltpu.SMEM)] + whole_specs(3 + len(panels)),
        out_specs=whole_specs(3),
        compiler_params=pltpu.CompilerParams(vmem_limit_bytes=14 * MIB),
    )(source, *gains, gathered, *panels)


def attend_pair(pair, pos, qkv, held):
    rows, columns = qkv[0].shape
    return pl.pallas_call(
        functools.partial(attend_kernel, pair),
        out_shape=jax.ShapeDtypeStruct((rows // 2, columns), jnp.bfloat16),
        in_specs=[pl.BlockSpec(memory_space=pltpu.SMEM)] + whole_specs(3 + len(held)),
        out_specs=whole_specs(1)[0],
        compiler_params=pltpu.CompilerParams(vmem_limit_bytes=10 * MIB),
    )(pos, *qkv, *held)


def mix_pair(pair, places, pos, gains, parts, panels, held):
    tile, head_dim = parts[0].shape[1], gains[0].shape[1]
    shape = (2 * tile, 2 * head_dim)
    return pl.pallas_call(
        functools.partial(both_kernel, pair, places),
        out_shape=jax.ShapeDtypeStruct(shape, jnp.bfloat16),
        in_specs=[pl.BlockSpec(memory_space=pltpu.SMEM)]
        + whole_specs(2 + len(parts))
        + [HBM_SPEC] * (len(panels) + len(held)),
        out_specs=whole_specs(1)[0],
        scratch_shapes=[
            pltpu.VMEM((len(panels), *panels[0].shape), jnp.bfloat16),
            pltpu.VMEM((len(held), *held[0].shape), jnp.bfloat16),
            *[pltpu.VMEM(shape, jnp.bfloat16)] * 3,
            pltpu.SemaphoreType.DMA((len(panels),)),
            pltpu.SemaphoreType.DMA((len(held),)),
        ],
        compiler_params=pltpu.CompilerParams(vmem_limit_bytes=16 * MIB),
    )(pos, *gains, *parts, *map(in_hbm, panels), *map(in_hbm, held))


def out_kernel(w_ref, *refs):
    mixed, (keep_ref, send_ref) = refs[:WAYS], refs[WAYS:]
    tile = keep_ref.shape[0]
    rows = jnp.concatenate([part[...] for part in mixed], axis=1)
    update = jnp.dot(rows, w_ref[...], preferred_element_type=jnp.float32)
    keep_ref[...] = update[:tile]
    send_ref[...] = update[tile:].astype(jnp.bfloat16)


def project_out(w_rows, mixed):
    shape = (mixed[0].shape[0] // 2, w_rows.shape[1])
    return pl.pallas_call(
        out_kernel,
        out_shape=[
            jax.ShapeDtypeStruct(shape, jnp.float32),
            jax.ShapeDtypeStruct(shape, jnp.bfloat16),
        ],
        in_specs=whole_specs(1 + WAYS),
        out_specs=whole_specs(2),
        compiler_params=pltpu.CompilerParams(vmem_limit_bytes=6 * MIB),
    )(w_rows, *mixed)


SWAP = [(0, 1), (1, 0)]


def from_z(value, k):
    return lax.ppermute(value, "cache", [(i, i ^ k) for i in range(WAYS)])


def split_heads(
    tokens,
    norm_gain,
    w_query,
    w_key,
    w_value,
    w_out,
    query_gain,
    key_gain,
    cache_keys,
    cache_values,
    step_gate,
    block_list,
    block_home,
    reader_span,
):
    z = lax.axis_index("cache")
    p = lax.axis_index(("fsdp", "head"))
    y = lax.axis_index("groups")
    head_dim = query_gain.shape[0]
    held_blocks = cache_keys.shape[0] // BLOCK
    width = tokens.shape[1] // WAYS
    tile = tokens.shape[0]
    ways = jnp.arange(WAYS, dtype=jnp.int32)

    def gather_pairs(by_z):
        low = jnp.stack(by_z[:2])
        low_x = lax.ppermute(low, "fsdp", SWAP)
        high = jnp.stack(by_z[2:])
        high_x = lax.ppermute(high, "fsdp", SWAP)
        mine = [low, high, low_x, high_x]
        low_c, high_c, low_xc, high_xc = [lax.ppermute(pair, "head", SWAP) for pair in mine]
        return [low, high, low_c, high_c, low_x, high_x, low_xc, high_xc]

    weights = (w_query, w_key, w_value)
    gain_lanes = jnp.broadcast_to(
        lax.dynamic_slice_in_dim(norm_gain, z * width, width, 0)[:, None], (width, head_dim)
    )
    order = (2, 3, 1)
    *sends, end = pack_panels([(k, 0) for k in order], gain_lanes, weights)
    sends = dict(zip(order, sends))
    near = {k: from_z(sends[k], k) for k in order}
    tokens, _ = lax.optimization_barrier((tokens, end))
    piece = lax.dynamic_slice_in_dim(tokens, p * width, width, 1)
    far_piece = from_z(piece, 2)
    parts = gather_pairs([piece, from_z(piece, 1), far_piece, from_z(far_piece, 1)])
    far = {k: lax.ppermute(near[k], "groups", SWAP) for k in order}
    packs = dict(zip((2, 3, 1, 0), pack_cache((2, 3, 1, 0), cache_keys, cache_values, head_dim)))
    held = [packs[0]]
    for k in range(1, WAYS):
        pack, _ = lax.optimization_barrier((packs[k], near[k]))
        held.append(from_z(pack, k))
    near[0], far[0], _ = pack_panels([(0, 0), (0, 1)], gain_lanes, weights)
    panels = [side[k] for k in range(WAYS) for side in (near, far)]
    gathered = jnp.concatenate(parts, axis=0)
    source = (z ^ p ^ ways)[None, :] * WAYS + (z ^ p ^ ways)[:, None]
    source = source.reshape(-1)
    x_share = lax.dynamic_index_in_dim(gathered, source[0], 0, keepdims=False)
    gains = (query_gain[None], key_gain[None])

    heads = jnp.stack([(z ^ ways) * 2 + y, (z ^ ways) * 2 + 1 - y], axis=1).reshape(-1)
    w_rows = jnp.take(w_out.reshape(2 * WAYS, head_dim, width), heads, axis=0).reshape(-1, width)
    gates = lax.dynamic_slice_in_dim(step_gate, z * width, width, 1)
    slots = jnp.take(block_home, jnp.take(block_list, jnp.take(reader_span, p ^ ways), axis=0))
    from_k = slots[:, :, None] // held_blocks == (z ^ ways)[None, None, :]
    pos = jnp.sum(jnp.where(from_k, (slots % held_blocks)[:, :, None], 0), axis=1).reshape(-1)

    def gather_z(own):
        near, far = lax.optimization_barrier((from_z(own, 1), from_z(own, 2)))
        return [own, near, far, from_z(far, 1)]

    def summed(mixed):
        keep, send = project_out(w_rows, mixed)
        return keep + lax.ppermute(send, "head", SWAP).astype(jnp.float32)

    qkv = project(source, gains, gathered, panels)
    mixed = gather_z(attend_pair(1, pos, qkv, held))
    pos_late, _ = lax.optimization_barrier((pos, mixed[0]))
    late = gather_z(attend_pair(0, pos_late, qkv, held))
    mixed[3], late[1], late[2] = lax.optimization_barrier((mixed[3], late[1], late[2]))
    other = summed(mixed).astype(jnp.bfloat16)
    other, late[3] = lax.optimization_barrier((other, late[3]))
    other = lax.ppermute(other, "fsdp", SWAP)
    update = summed(late) + other.astype(jnp.float32)
    x_share = (x_share.astype(jnp.float32) + gates[0] * update).astype(jnp.bfloat16)

    near, far, own_x = lax.optimization_barrier(
        (from_z(x_share, 1), from_z(x_share, 2), lax.ppermute(x_share[None], "fsdp", SWAP))
    )
    last = from_z(far, 1)
    by_z = [jnp.stack([x_share, near]), jnp.stack([far, last])]
    by_z += [lax.ppermute(part, "head", SWAP) for part in by_z]
    by_x = [own_x, *[lax.ppermute(v, "fsdp", SWAP) for v in (jnp.stack([near, far]), last[None])]]
    own = mix_pair(0, ((0, 0), (0, 1), (1, 0), (1, 1)), pos, gains, by_z, panels, held)
    first = gather_z(own)
    by_x[1], by_x[2], first[0] = lax.optimization_barrier((by_x[1], by_x[2], first[0]))
    by_x += [lax.ppermute(part, "head", SWAP) for part in by_x]
    second = gather_z(
        mix_pair(1, ((0, 0), (1, 0), (1, 1), (2, 0)), pos, gains, by_x, panels, held)
    )
    values = [x_share.astype(jnp.float32) + gates[1] * summed(first), gates[1] * summed(second)]
    ends = [
        lax.ppermute(
            value.astype(jnp.bfloat16),
            ("cache", "fsdp", "head"),
            [(a * WAYS + b, (b ^ flip) * WAYS + a) for a in range(WAYS) for b in range(WAYS)],
        ).astype(jnp.float32)
        for value, flip in zip(values, (0, 2))
    ]
    return (ends[0] + ends[1]).astype(jnp.bfloat16)


def solution(mesh):
    in_specs = (
        P(("groups", "cache"), None),
        P(),
        P("cache", ("fsdp", "head")),
        P("cache", ("fsdp", "head")),
        P("cache", ("fsdp", "head")),
        P(("fsdp", "head"), "cache"),
        P(),
        P(),
        P(("groups", "cache"), ("fsdp", "head")),
        P(("groups", "cache"), ("fsdp", "head")),
        P(),
        P("groups", None),
        P("groups"),
        P("groups"),
    )
    out_specs = P(("groups", "cache"), ("fsdp", "head"))
    sizes = dict(mesh.shape)

    def program(*args):
        panel_width, head_dim = args[2].shape[1] // (sizes["fsdp"] * sizes["head"]), args[6].shape[0]
        fits = (
            sizes == {"groups": 2, "cache": WAYS, "fsdp": 2, "head": 2}
            and panel_width == 2 * WAYS * head_dim
            and args[11].shape[1] == WAYS
            and ITERS == 2
        )
        plan = split_heads if fits else gathered_panels
        return jax.shard_map(
            plan, mesh=mesh, in_specs=in_specs, out_specs=out_specs, check_vma=False
        )(*args)

    return program
```

```python
import functools

import jax
import jax.numpy as jnp
from jax import lax
from jax.experimental import pallas as pl
from jax.experimental.pallas import tpu as pltpu
from jax.sharding import PartitionSpec as P

BLOCK = 256
ITERS = 2


epsilon = 1e-06


def rms_scale(values, gain_row):
    mean_square = jnp.mean(values * values, axis=-1, keepdims=True)
    return values * lax.rsqrt(mean_square + epsilon) * gain_row


def head_norm(projected, gain_row):
    row_count = projected.shape[0]
    split = projected.reshape(row_count, -1, gain_row.shape[0])
    return rms_scale(split, gain_row).astype(jnp.bfloat16).reshape(row_count, -1)


def attend(queries, key_rows, value_rows, head_dim):
    row_count = queries.shape[0]
    head_count = queries.shape[1] // head_dim
    query_heads = queries.reshape(row_count, head_count, head_dim)
    key_heads = key_rows.reshape(-1, head_count, head_dim)
    value_heads = value_rows.reshape(-1, head_count, head_dim)
    scores = jnp.einsum(
        "qhd,khd->hqk", query_heads, key_heads, preferred_element_type=jnp.float32
    ) * head_dim ** (-0.5)
    weights = jnp.exp(scores)
    totals = jnp.sum(weights, axis=2)
    summed = jnp.einsum(
        "hqk,khd->qhd",
        weights.astype(jnp.bfloat16),
        value_heads,
        preferred_element_type=jnp.float32,
    )
    return (
        (summed / jnp.transpose(totals)[:, :, None])
        .astype(jnp.bfloat16)
        .reshape(row_count, head_count * head_dim)
    )


def gathered_panels(
    tokens,
    norm_gain,
    w_query,
    w_key,
    w_value,
    w_out,
    query_gain,
    key_gain,
    cache_keys,
    cache_values,
    step_gate,
    block_list,
    block_home,
    reader_span,
):
    reader_index = lax.axis_index("cache")
    group_index = lax.axis_index(("fsdp", "head"))
    head_dim = query_gain.shape[0]
    panel_width = cache_keys.shape[1]
    held_blocks = cache_keys.shape[0] // BLOCK
    full_query, full_key, full_value = (
        lax.all_gather(w_query, "cache", axis=0, tiled=True),
        lax.all_gather(w_key, "cache", axis=0, tiled=True),
        lax.all_gather(w_value, "cache", axis=0, tiled=True),
    )
    out_panel = lax.all_gather(w_out, "cache", axis=1, tiled=True)
    wanted = jnp.take(block_list, reader_span, axis=0)
    home_slots = jnp.take(block_home, wanted)
    is_mine = home_slots // held_blocks == reader_index
    local_pos = jnp.sum(jnp.where(is_mine, home_slots % held_blocks, 0), axis=1)
    key_blocks = cache_keys.reshape(held_blocks, BLOCK, panel_width)
    value_blocks = cache_values.reshape(held_blocks, BLOCK, panel_width)
    send_keys = jnp.take(key_blocks, local_pos, axis=0)
    send_values = jnp.take(value_blocks, local_pos, axis=0)
    got_keys, got_values = (
        lax.all_to_all(send_keys, "cache", split_axis=0, concat_axis=0, tiled=True),
        lax.all_to_all(send_values, "cache", split_axis=0, concat_axis=0, tiled=True),
    )
    my_span = jnp.take(reader_span, reader_index)
    my_owners = jnp.take(block_home, jnp.take(block_list, my_span, axis=0)) // held_blocks
    fetched_keys = jnp.take(got_keys, my_owners, axis=0).reshape(-1, panel_width)
    fetched_values = jnp.take(got_values, my_owners, axis=0).reshape(-1, panel_width)
    out_columns = lax.all_to_all(
        out_panel, ("fsdp", "head"), split_axis=1, concat_axis=0, tiled=True
    )
    column_count = tokens.shape[1] // lax.axis_size(("fsdp", "head"))
    column_start = group_index * column_count
    current = tokens
    x_share = lax.dynamic_slice_in_dim(tokens, column_start, column_count, 1)
    for step_index in range(ITERS):
        normed = rms_scale(current.astype(jnp.float32), norm_gain).astype(jnp.bfloat16)
        queries = head_norm(
            jnp.dot(normed, full_query, preferred_element_type=jnp.float32), query_gain
        )
        own_keys = head_norm(
            jnp.dot(normed, full_key, preferred_element_type=jnp.float32), key_gain
        )
        own_values = jnp.dot(normed, full_value, preferred_element_type=jnp.float32).astype(
            jnp.bfloat16
        )
        all_keys = jnp.concatenate([fetched_keys, own_keys], axis=0)
        all_values = jnp.concatenate([fetched_values, own_values], axis=0)
        mixed = attend(queries, all_keys, all_values, head_dim)
        step_scale = step_gate[step_index]
        share_scale = lax.dynamic_slice_in_dim(step_scale, column_start, column_count, 0)
        heads_all = lax.all_gather(mixed, ("fsdp", "head"), axis=1, tiled=True)
        update = jnp.dot(heads_all, out_columns, preferred_element_type=jnp.float32)
        x_share = (x_share.astype(jnp.float32) + share_scale * update).astype(jnp.bfloat16)
        if step_index + 1 < ITERS:
            current = lax.all_gather(x_share, ("fsdp", "head"), axis=1, tiled=True)
    return x_share


WAYS = 4
MIB = 1024 * 1024


def in_hbm(value):
    return pltpu.with_memory_space_constraint(value, pltpu.HBM)


HBM_SPEC = pl.BlockSpec(memory_space=pltpu.HBM)


def whole_specs(count):
    return [pl.BlockSpec(memory_space=pltpu.VMEM) for _ in range(count)]


def head_lanes(k, h, head_dim):
    z, y = lax.axis_index("cache"), lax.axis_index("groups")
    return pl.ds(pl.multiple_of(((z ^ k) * 2 + (y ^ h)) * head_dim, head_dim), head_dim)


def pack_panels_kernel(slots, gain_ref, *refs):
    weights, panels, (end_ref, held_ref, sems) = refs[:3], refs[3:-3], refs[-3:]
    end_ref[...] = jnp.zeros_like(end_ref)
    head_dim = gain_ref.shape[1]
    copies = []
    for i, (k, h) in enumerate(slots):
        for m, weight in enumerate(weights):
            copies.append(
                pltpu.make_async_copy(
                    weight.at[:, head_lanes(k, h, head_dim)],
                    held_ref.at[i, :, m * head_dim : (m + 1) * head_dim],
                    sems.at[i * 3 + m],
                )
            )
            copies[-1].start()
    for i, panel in enumerate(panels):
        for m in range(3):
            copies[i * 3 + m].wait()
            lanes = slice(m * head_dim, (m + 1) * head_dim)
            panel[:, lanes] = (held_ref[i, :, lanes].astype(jnp.float32) * gain_ref[...]).astype(
                jnp.bfloat16
            )


def pack_panels(slots, gain_lanes, weights):
    depth, head_dim = gain_lanes.shape
    shape = jax.ShapeDtypeStruct((depth, 3 * head_dim), jnp.bfloat16)
    return pl.pallas_call(
        functools.partial(pack_panels_kernel, slots),
        out_shape=[shape] * len(slots) + [jax.ShapeDtypeStruct((8, head_dim), jnp.float32)],
        in_specs=whole_specs(1) + [HBM_SPEC] * 3,
        out_specs=whole_specs(len(slots) + 1),
        scratch_shapes=[
            pltpu.VMEM((len(slots), depth, 3 * head_dim), jnp.bfloat16),
            pltpu.SemaphoreType.DMA((3 * len(slots),)),
        ],
        compiler_params=pltpu.CompilerParams(vmem_limit_bytes=10 * MIB),
    )(gain_lanes, *[in_hbm(w) for w in weights])


def pack_cache_kernel(ks, keys_ref, values_ref, *refs):
    packs, sems = refs[:-1], refs[-1]
    head_dim = packs[0].shape[1] // 4
    copies = []
    for i, (k, pack) in enumerate(zip(ks, packs)):
        for m in range(4):
            source = (keys_ref, values_ref)[m // 2]
            copies.append(
                pltpu.make_async_copy(
                    source.at[:, head_lanes(k, m % 2, head_dim)],
                    pack.at[:, m * head_dim : (m + 1) * head_dim],
                    sems.at[i * 4 + m],
                )
            )
            copies[-1].start()
    for copy in copies:
        copy.wait()


def pack_cache(ks, keys, values, head_dim):
    shape = jax.ShapeDtypeStruct((keys.shape[0], 4 * head_dim), jnp.bfloat16)
    return pl.pallas_call(
        functools.partial(pack_cache_kernel, ks),
        out_shape=[shape] * len(ks),
        in_specs=[HBM_SPEC] * 2,
        out_specs=whole_specs(len(ks)),
        scratch_shapes=[pltpu.SemaphoreType.DMA((4 * len(ks),))],
        compiler_params=pltpu.CompilerParams(vmem_limit_bytes=6 * MIB),
    )(*map(in_hbm, (keys, values)))


def project_rows(tiles, part, panel, query_gain_ref, key_gain_ref, outs):
    q_ref, k_ref, v_ref = outs
    head_dim = query_gain_ref.shape[1]
    totals = [None, None]
    squares = [0.0] * tiles
    columns = 0
    for k in range(WAYS):
        blocks = [part(r, k) for r in range(tiles)]
        rows = jnp.concatenate(blocks, axis=0)
        columns += rows.shape[1]
        for h in range(2):
            product = jnp.dot(rows, panel(k, h), preferred_element_type=jnp.float32)
            totals[h] = product if k == 0 else totals[h] + product
        for r in range(tiles):
            wide = blocks[r].astype(jnp.float32)
            squares[r] += jnp.sum(wide * wide, axis=-1, keepdims=True)
    scale = lax.rsqrt(jnp.concatenate(squares, axis=0) / columns + epsilon)
    for h in range(2):
        total = totals[h] * scale
        lanes = slice(h * head_dim, (h + 1) * head_dim)
        q_ref[:, lanes] = rms_scale(total[:, :head_dim], query_gain_ref[...]).astype(jnp.bfloat16)
        k_ref[:, lanes] = rms_scale(
            total[:, head_dim : 2 * head_dim], key_gain_ref[...]
        ).astype(jnp.bfloat16)
        v_ref[:, lanes] = total[:, 2 * head_dim :].astype(jnp.bfloat16)


def attend_rows(pair, start, pos_ref, q_ref, k_ref, v_ref, held, mixed_ref):
    head_dim = q_ref.shape[1] // 2
    tile = mixed_ref.shape[0] // 2
    across = (((1,), (1,)), ((), ()))
    for h in range(2):
        for r in range(2 * pair, 2 * pair + 2):
            at = (r - 2 * pair) * tile
            rows = slice(start + at, start + at + tile)
            lanes = slice(h * head_dim, (h + 1) * head_dim)
            value_lanes = slice((2 + h) * head_dim, (3 + h) * head_dim)
            query = q_ref[rows, lanes]
            keys = [k_ref[rows, lanes]]
            values = [v_ref[rows, lanes]]
            for k in range(WAYS):
                block = pl.ds(pl.multiple_of(pos_ref[r * WAYS + k] * BLOCK, BLOCK), BLOCK)
                keys.append(held[k][block, lanes])
                values.append(held[k][block, value_lanes])
            total = jnp.zeros((tile, 1), jnp.float32)
            summed = jnp.zeros((tile, head_dim), jnp.float32)
            for key, value in zip(keys, values):
                scores = lax.dot_general(query, key, across, preferred_element_type=jnp.float32)
                weights = jnp.exp(scores * head_dim ** (-0.5))
                total += jnp.sum(weights, axis=-1, keepdims=True)
                summed += jnp.dot(
                    weights.astype(jnp.bfloat16), value, preferred_element_type=jnp.float32
                )
            mixed_ref[at : at + tile, lanes] = (summed / total).astype(jnp.bfloat16)


def project_kernel(source_ref, query_gain_ref, key_gain_ref, gathered_ref, *refs):
    panels, outs = refs[: 2 * WAYS], refs[2 * WAYS :]

    def part(j, k):
        return gathered_ref[source_ref[j * WAYS + k]]

    def panel(k, h):
        return panels[2 * k + h][...]

    project_rows(WAYS, part, panel, query_gain_ref, key_gain_ref, outs)


def attend_kernel(pair, pos_ref, q_ref, k_ref, v_ref, *refs):
    start = pair * refs[WAYS].shape[0]
    attend_rows(pair, start, pos_ref, q_ref, k_ref, v_ref, refs[:WAYS], refs[WAYS])


def mix_rows(pair, places, parts, panel, held, pos_ref, query_gain_ref, key_gain_ref, outs, mixed_ref):
    count = len(parts) // 2

    def part(j, k):
        at, inner = places[k]
        return parts[j * count + at][inner]

    project_rows(2, part, panel, query_gain_ref, key_gain_ref, outs)
    attend_rows(pair, 0, pos_ref, *outs, held(), mixed_ref)


def mix_own_kernel(places, pos_ref, query_gain_ref, key_gain_ref, *refs):
    parts, panels, caches = refs[:WAYS], refs[WAYS : 3 * WAYS], refs[3 * WAYS : 4 * WAYS]
    mixed_ref, panel_ref, held_ref, *outs, panel_sems, held_sems = refs[4 * WAYS :]
    copies = [
        pltpu.make_async_copy(source, panel_ref.at[i], panel_sems.at[i])
        for i, source in enumerate(panels)
    ]
    late = [
        pltpu.make_async_copy(source, held_ref.at[i], held_sems.at[i])
        for i, source in enumerate(caches)
    ]
    for copy in copies + late:
        copy.start()

    def panel(k, h):
        copies[2 * k + h].wait()
        return panel_ref[2 * k + h]

    def held():
        for copy in late:
            copy.wait()
        return [held_ref.at[k] for k in range(WAYS)]

    mix_rows(0, places, parts, panel, held, pos_ref, query_gain_ref, key_gain_ref, outs, mixed_ref)


def mix_other_kernel(places, pos_ref, query_gain_ref, key_gain_ref, *refs):
    *parts, panel_ref, held_ref, mixed_ref, q_ref, k_ref, v_ref = refs

    def panel(k, h):
        return panel_ref[2 * k + h]

    def held():
        return [held_ref.at[k] for k in range(WAYS)]

    outs = (q_ref, k_ref, v_ref)
    mix_rows(1, places, parts, panel, held, pos_ref, query_gain_ref, key_gain_ref, outs, mixed_ref)


def project(source, gains, gathered, panels):
    tile, head_dim = gathered.shape[1], gains[0].shape[1]
    return pl.pallas_call(
        project_kernel,
        out_shape=[jax.ShapeDtypeStruct((WAYS * tile, 2 * head_dim), jnp.bfloat16)] * 3,
        in_specs=[pl.BlockSpec(memory_space=pltpu.SMEM)] + whole_specs(3 + len(panels)),
        out_specs=whole_specs(3),
        compiler_params=pltpu.CompilerParams(vmem_limit_bytes=14 * MIB),
    )(source, *gains, gathered, *panels)


def attend_pair(pair, pos, qkv, held):
    rows, columns = qkv[0].shape
    return pl.pallas_call(
        functools.partial(attend_kernel, pair),
        out_shape=jax.ShapeDtypeStruct((rows // 2, columns), jnp.bfloat16),
        in_specs=[pl.BlockSpec(memory_space=pltpu.SMEM)] + whole_specs(3 + len(held)),
        out_specs=whole_specs(1)[0],
        compiler_params=pltpu.CompilerParams(vmem_limit_bytes=10 * MIB),
    )(pos, *qkv, *held)


def mix_own(places, pos, gains, parts, panels, held):
    tile, head_dim = parts[0].shape[1], gains[0].shape[1]
    shape = (2 * tile, 2 * head_dim)
    return pl.pallas_call(
        functools.partial(mix_own_kernel, places),
        out_shape=[
            jax.ShapeDtypeStruct(shape, jnp.bfloat16),
            jax.ShapeDtypeStruct((len(panels), *panels[0].shape), jnp.bfloat16),
            jax.ShapeDtypeStruct((len(held), *held[0].shape), jnp.bfloat16),
        ],
        in_specs=[pl.BlockSpec(memory_space=pltpu.SMEM)]
        + whole_specs(2 + len(parts))
        + [HBM_SPEC] * (len(panels) + len(held)),
        out_specs=whole_specs(3),
        scratch_shapes=[
            *[pltpu.VMEM(shape, jnp.bfloat16)] * 3,
            pltpu.SemaphoreType.DMA((len(panels),)),
            pltpu.SemaphoreType.DMA((len(held),)),
        ],
        compiler_params=pltpu.CompilerParams(vmem_limit_bytes=16 * MIB),
    )(pos, *gains, *parts, *map(in_hbm, panels), *map(in_hbm, held))


def mix_other(places, pos, gains, parts, panels, held):
    tile, head_dim = parts[0].shape[1], gains[0].shape[1]
    shape = (2 * tile, 2 * head_dim)
    return pl.pallas_call(
        functools.partial(mix_other_kernel, places),
        out_shape=jax.ShapeDtypeStruct(shape, jnp.bfloat16),
        in_specs=[pl.BlockSpec(memory_space=pltpu.SMEM)] + whole_specs(4 + len(parts)),
        out_specs=whole_specs(1)[0],
        scratch_shapes=[pltpu.VMEM(shape, jnp.bfloat16)] * 3,
        compiler_params=pltpu.CompilerParams(vmem_limit_bytes=16 * MIB),
    )(pos, *gains, *parts, panels, held)


def out_kernel(w_ref, *refs):
    mixed, (keep_ref, send_ref) = refs[:WAYS], refs[WAYS:]
    tile = keep_ref.shape[0]
    rows = jnp.concatenate([part[...] for part in mixed], axis=1)
    update = jnp.dot(rows, w_ref[...], preferred_element_type=jnp.float32)
    keep_ref[...] = update[:tile]
    send_ref[...] = update[tile:].astype(jnp.bfloat16)


def project_out(w_rows, mixed):
    shape = (mixed[0].shape[0] // 2, w_rows.shape[1])
    return pl.pallas_call(
        out_kernel,
        out_shape=[
            jax.ShapeDtypeStruct(shape, jnp.float32),
            jax.ShapeDtypeStruct(shape, jnp.bfloat16),
        ],
        in_specs=whole_specs(1 + WAYS),
        out_specs=whole_specs(2),
        compiler_params=pltpu.CompilerParams(vmem_limit_bytes=6 * MIB),
    )(w_rows, *mixed)


SWAP = [(0, 1), (1, 0)]


def from_z(value, k):
    return lax.ppermute(value, "cache", [(i, i ^ k) for i in range(WAYS)])


def split_heads(
    tokens,
    norm_gain,
    w_query,
    w_key,
    w_value,
    w_out,
    query_gain,
    key_gain,
    cache_keys,
    cache_values,
    step_gate,
    block_list,
    block_home,
    reader_span,
):
    z = lax.axis_index("cache")
    p = lax.axis_index(("fsdp", "head"))
    y = lax.axis_index("groups")
    head_dim = query_gain.shape[0]
    held_blocks = cache_keys.shape[0] // BLOCK
    width = tokens.shape[1] // WAYS
    tile = tokens.shape[0]
    ways = jnp.arange(WAYS, dtype=jnp.int32)

    def gather_pairs(by_z):
        low = jnp.stack(by_z[:2])
        low_x = lax.ppermute(low, "fsdp", SWAP)
        high = jnp.stack(by_z[2:])
        high_x = lax.ppermute(high, "fsdp", SWAP)
        mine = [low, high, low_x, high_x]
        low_c, high_c, low_xc, high_xc = [lax.ppermute(pair, "head", SWAP) for pair in mine]
        return [low, high, low_c, high_c, low_x, high_x, low_xc, high_xc]

    weights = (w_query, w_key, w_value)
    gain_lanes = jnp.broadcast_to(
        lax.dynamic_slice_in_dim(norm_gain, z * width, width, 0)[:, None], (width, head_dim)
    )
    order = (2, 3, 1)
    *sends, end = pack_panels([(k, 0) for k in order], gain_lanes, weights)
    sends = dict(zip(order, sends))
    near = {k: from_z(sends[k], k) for k in order}
    tokens, _ = lax.optimization_barrier((tokens, end))
    piece = lax.dynamic_slice_in_dim(tokens, p * width, width, 1)
    far_piece = from_z(piece, 2)
    parts = gather_pairs([piece, from_z(piece, 1), far_piece, from_z(far_piece, 1)])
    far = {k: lax.ppermute(near[k], "groups", SWAP) for k in order}
    packs = dict(zip((2, 3, 1, 0), pack_cache((2, 3, 1, 0), cache_keys, cache_values, head_dim)))
    held = [packs[0]]
    for k in range(1, WAYS):
        pack, _ = lax.optimization_barrier((packs[k], near[k]))
        held.append(from_z(pack, k))
    near[0], far[0], _ = pack_panels([(0, 0), (0, 1)], gain_lanes, weights)
    panels = [side[k] for k in range(WAYS) for side in (near, far)]
    gathered = jnp.concatenate(parts, axis=0)
    source = (z ^ p ^ ways)[None, :] * WAYS + (z ^ p ^ ways)[:, None]
    source = source.reshape(-1)
    x_share = lax.dynamic_index_in_dim(gathered, source[0], 0, keepdims=False)
    gains = (query_gain[None], key_gain[None])

    heads = jnp.stack([(z ^ ways) * 2 + y, (z ^ ways) * 2 + 1 - y], axis=1).reshape(-1)
    w_rows = jnp.take(w_out.reshape(2 * WAYS, head_dim, width), heads, axis=0).reshape(-1, width)
    gates = lax.dynamic_slice_in_dim(step_gate, z * width, width, 1)
    slots = jnp.take(block_home, jnp.take(block_list, jnp.take(reader_span, p ^ ways), axis=0))
    from_k = slots[:, :, None] // held_blocks == (z ^ ways)[None, None, :]
    pos = jnp.sum(jnp.where(from_k, (slots % held_blocks)[:, :, None], 0), axis=1).reshape(-1)

    def gather_z(own):
        near, far = lax.optimization_barrier((from_z(own, 1), from_z(own, 2)))
        return [own, near, far, from_z(far, 1)]

    def summed(mixed):
        keep, send = project_out(w_rows, mixed)
        return keep + lax.ppermute(send, "head", SWAP).astype(jnp.float32)

    qkv = project(source, gains, gathered, panels)
    mixed = gather_z(attend_pair(1, pos, qkv, held))
    pos_late, _ = lax.optimization_barrier((pos, mixed[0]))
    late = gather_z(attend_pair(0, pos_late, qkv, held))
    mixed[3], late[1], late[2] = lax.optimization_barrier((mixed[3], late[1], late[2]))
    other = summed(mixed).astype(jnp.bfloat16)
    other, late[3] = lax.optimization_barrier((other, late[3]))
    other = lax.ppermute(other, "fsdp", SWAP)
    update = summed(late) + other.astype(jnp.float32)
    x_share = (x_share.astype(jnp.float32) + gates[0] * update).astype(jnp.bfloat16)

    near, far, own_x = lax.optimization_barrier(
        (from_z(x_share, 1), from_z(x_share, 2), lax.ppermute(x_share[None], "fsdp", SWAP))
    )
    last = from_z(far, 1)
    by_z = [jnp.stack([x_share, near]), jnp.stack([far, last])]
    by_z += [lax.ppermute(part, "head", SWAP) for part in by_z]
    by_x = [own_x, *[lax.ppermute(v, "fsdp", SWAP) for v in (jnp.stack([near, far]), last[None])]]
    places = ((0, 0), (0, 1), (1, 0), (1, 1))
    own, panels, held = mix_own(places, pos, gains, by_z, panels, held)
    first = gather_z(own)
    by_x[1], by_x[2], first[0] = lax.optimization_barrier((by_x[1], by_x[2], first[0]))
    by_x += [lax.ppermute(part, "head", SWAP) for part in by_x]
    places = ((0, 0), (1, 0), (1, 1), (2, 0))
    second = gather_z(mix_other(places, pos, gains, by_x, panels, held))
    values = [x_share.astype(jnp.float32) + gates[1] * summed(first), gates[1] * summed(second)]
    ends = [
        lax.ppermute(
            value.astype(jnp.bfloat16),
            ("cache", "fsdp", "head"),
            [(a * WAYS + b, (b ^ flip) * WAYS + a) for a in range(WAYS) for b in range(WAYS)],
        ).astype(jnp.float32)
        for value, flip in zip(values, (0, 2))
    ]
    return (ends[0] + ends[1]).astype(jnp.bfloat16)


def solution(mesh):
    in_specs = (
        P(("groups", "cache"), None),
        P(),
        P("cache", ("fsdp", "head")),
        P("cache", ("fsdp", "head")),
        P("cache", ("fsdp", "head")),
        P(("fsdp", "head"), "cache"),
        P(),
        P(),
        P(("groups", "cache"), ("fsdp", "head")),
        P(("groups", "cache"), ("fsdp", "head")),
        P(),
        P("groups", None),
        P("groups"),
        P("groups"),
    )
    out_specs = P(("groups", "cache"), ("fsdp", "head"))
    sizes = dict(mesh.shape)

    def program(*args):
        panel_width, head_dim = args[2].shape[1] // (sizes["fsdp"] * sizes["head"]), args[6].shape[0]
        fits = (
            sizes == {"groups": 2, "cache": WAYS, "fsdp": 2, "head": 2}
            and panel_width == 2 * WAYS * head_dim
            and args[11].shape[1] == WAYS
            and ITERS == 2
        )
        plan = split_heads if fits else gathered_panels
        return jax.shard_map(
            plan, mesh=mesh, in_specs=in_specs, out_specs=out_specs, check_vma=False
        )(*args)

    return program
```

```python
import functools

import jax
import jax.numpy as jnp
from jax import lax
from jax.experimental import pallas as pl
from jax.experimental.pallas import tpu as pltpu
from jax.sharding import PartitionSpec as P

BLOCK = 256
ITERS = 2


epsilon = 1e-06


def rms_scale(values, gain_row):
    mean_square = jnp.mean(values * values, axis=-1, keepdims=True)
    return values * lax.rsqrt(mean_square + epsilon) * gain_row


def head_norm(projected, gain_row):
    row_count = projected.shape[0]
    split = projected.reshape(row_count, -1, gain_row.shape[0])
    return rms_scale(split, gain_row).astype(jnp.bfloat16).reshape(row_count, -1)


def attend(queries, key_rows, value_rows, head_dim):
    row_count = queries.shape[0]
    head_count = queries.shape[1] // head_dim
    query_heads = queries.reshape(row_count, head_count, head_dim)
    key_heads = key_rows.reshape(-1, head_count, head_dim)
    value_heads = value_rows.reshape(-1, head_count, head_dim)
    scores = jnp.einsum(
        "qhd,khd->hqk", query_heads, key_heads, preferred_element_type=jnp.float32
    ) * head_dim ** (-0.5)
    weights = jnp.exp(scores)
    totals = jnp.sum(weights, axis=2)
    summed = jnp.einsum(
        "hqk,khd->qhd",
        weights.astype(jnp.bfloat16),
        value_heads,
        preferred_element_type=jnp.float32,
    )
    return (
        (summed / jnp.transpose(totals)[:, :, None])
        .astype(jnp.bfloat16)
        .reshape(row_count, head_count * head_dim)
    )


def gathered_panels(
    tokens,
    norm_gain,
    w_query,
    w_key,
    w_value,
    w_out,
    query_gain,
    key_gain,
    cache_keys,
    cache_values,
    step_gate,
    block_list,
    block_home,
    reader_span,
):
    reader_index = lax.axis_index("cache")
    group_index = lax.axis_index(("fsdp", "head"))
    head_dim = query_gain.shape[0]
    panel_width = cache_keys.shape[1]
    held_blocks = cache_keys.shape[0] // BLOCK
    full_query, full_key, full_value = (
        lax.all_gather(w_query, "cache", axis=0, tiled=True),
        lax.all_gather(w_key, "cache", axis=0, tiled=True),
        lax.all_gather(w_value, "cache", axis=0, tiled=True),
    )
    out_panel = lax.all_gather(w_out, "cache", axis=1, tiled=True)
    wanted = jnp.take(block_list, reader_span, axis=0)
    home_slots = jnp.take(block_home, wanted)
    is_mine = home_slots // held_blocks == reader_index
    local_pos = jnp.sum(jnp.where(is_mine, home_slots % held_blocks, 0), axis=1)
    key_blocks = cache_keys.reshape(held_blocks, BLOCK, panel_width)
    value_blocks = cache_values.reshape(held_blocks, BLOCK, panel_width)
    send_keys = jnp.take(key_blocks, local_pos, axis=0)
    send_values = jnp.take(value_blocks, local_pos, axis=0)
    got_keys, got_values = (
        lax.all_to_all(send_keys, "cache", split_axis=0, concat_axis=0, tiled=True),
        lax.all_to_all(send_values, "cache", split_axis=0, concat_axis=0, tiled=True),
    )
    my_span = jnp.take(reader_span, reader_index)
    my_owners = jnp.take(block_home, jnp.take(block_list, my_span, axis=0)) // held_blocks
    fetched_keys = jnp.take(got_keys, my_owners, axis=0).reshape(-1, panel_width)
    fetched_values = jnp.take(got_values, my_owners, axis=0).reshape(-1, panel_width)
    out_columns = lax.all_to_all(
        out_panel, ("fsdp", "head"), split_axis=1, concat_axis=0, tiled=True
    )
    column_count = tokens.shape[1] // lax.axis_size(("fsdp", "head"))
    column_start = group_index * column_count
    current = tokens
    x_share = lax.dynamic_slice_in_dim(tokens, column_start, column_count, 1)
    for step_index in range(ITERS):
        normed = rms_scale(current.astype(jnp.float32), norm_gain).astype(jnp.bfloat16)
        queries = head_norm(
            jnp.dot(normed, full_query, preferred_element_type=jnp.float32), query_gain
        )
        own_keys = head_norm(
            jnp.dot(normed, full_key, preferred_element_type=jnp.float32), key_gain
        )
        own_values = jnp.dot(normed, full_value, preferred_element_type=jnp.float32).astype(
            jnp.bfloat16
        )
        all_keys = jnp.concatenate([fetched_keys, own_keys], axis=0)
        all_values = jnp.concatenate([fetched_values, own_values], axis=0)
        mixed = attend(queries, all_keys, all_values, head_dim)
        step_scale = step_gate[step_index]
        share_scale = lax.dynamic_slice_in_dim(step_scale, column_start, column_count, 0)
        heads_all = lax.all_gather(mixed, ("fsdp", "head"), axis=1, tiled=True)
        update = jnp.dot(heads_all, out_columns, preferred_element_type=jnp.float32)
        x_share = (x_share.astype(jnp.float32) + share_scale * update).astype(jnp.bfloat16)
        if step_index + 1 < ITERS:
            current = lax.all_gather(x_share, ("fsdp", "head"), axis=1, tiled=True)
    return x_share


WAYS = 4
MIB = 1024 * 1024


def in_hbm(value):
    return pltpu.with_memory_space_constraint(value, pltpu.HBM)


HBM_SPEC = pl.BlockSpec(memory_space=pltpu.HBM)


def whole_specs(count):
    return [pl.BlockSpec(memory_space=pltpu.VMEM) for _ in range(count)]


def head_lanes(k, h, head_dim):
    z, y = lax.axis_index("cache"), lax.axis_index("groups")
    return pl.ds(pl.multiple_of(((z ^ k) * 2 + (y ^ h)) * head_dim, head_dim), head_dim)


def pack_panels_kernel(slots, gain_ref, *refs):
    weights, panels, (end_ref, held_ref, sems) = refs[:3], refs[3:-3], refs[-3:]
    end_ref[...] = jnp.zeros_like(end_ref)
    head_dim = gain_ref.shape[1]
    copies = []
    for i, (k, h) in enumerate(slots):
        for m, weight in enumerate(weights):
            copies.append(
                pltpu.make_async_copy(
                    weight.at[:, head_lanes(k, h, head_dim)],
                    held_ref.at[i, :, m * head_dim : (m + 1) * head_dim],
                    sems.at[i * 3 + m],
                )
            )
            copies[-1].start()
    for i, panel in enumerate(panels):
        for m in range(3):
            copies[i * 3 + m].wait()
            lanes = slice(m * head_dim, (m + 1) * head_dim)
            panel[:, lanes] = (held_ref[i, :, lanes].astype(jnp.float32) * gain_ref[...]).astype(
                jnp.bfloat16
            )


def pack_panels(slots, gain_lanes, weights):
    depth, head_dim = gain_lanes.shape
    shape = jax.ShapeDtypeStruct((depth, 3 * head_dim), jnp.bfloat16)
    return pl.pallas_call(
        functools.partial(pack_panels_kernel, slots),
        out_shape=[shape] * len(slots) + [jax.ShapeDtypeStruct((8, head_dim), jnp.float32)],
        in_specs=whole_specs(1) + [HBM_SPEC] * 3,
        out_specs=whole_specs(len(slots) + 1),
        scratch_shapes=[
            pltpu.VMEM((len(slots), depth, 3 * head_dim), jnp.bfloat16),
            pltpu.SemaphoreType.DMA((3 * len(slots),)),
        ],
        compiler_params=pltpu.CompilerParams(vmem_limit_bytes=10 * MIB),
    )(gain_lanes, *[in_hbm(w) for w in weights])


def pack_cache_kernel(ks, keys_ref, values_ref, *refs):
    packs, sems = refs[:-1], refs[-1]
    head_dim = packs[0].shape[1] // 4
    copies = []
    for i, (k, pack) in enumerate(zip(ks, packs)):
        for m in range(4):
            source = (keys_ref, values_ref)[m // 2]
            copies.append(
                pltpu.make_async_copy(
                    source.at[:, head_lanes(k, m % 2, head_dim)],
                    pack.at[:, m * head_dim : (m + 1) * head_dim],
                    sems.at[i * 4 + m],
                )
            )
            copies[-1].start()
    for copy in copies:
        copy.wait()


def pack_cache(ks, keys, values, head_dim):
    shape = jax.ShapeDtypeStruct((keys.shape[0], 4 * head_dim), jnp.bfloat16)
    return pl.pallas_call(
        functools.partial(pack_cache_kernel, ks),
        out_shape=[shape] * len(ks),
        in_specs=[HBM_SPEC] * 2,
        out_specs=whole_specs(len(ks)),
        scratch_shapes=[pltpu.SemaphoreType.DMA((4 * len(ks),))],
        compiler_params=pltpu.CompilerParams(vmem_limit_bytes=6 * MIB),
    )(*map(in_hbm, (keys, values)))


def project_rows(tiles, part, panel, query_gain_ref, key_gain_ref, outs):
    q_ref, k_ref, v_ref = outs
    head_dim = query_gain_ref.shape[1]
    totals = [None, None]
    squares = [0.0] * tiles
    columns = 0
    for k in range(WAYS):
        blocks = [part(r, k) for r in range(tiles)]
        rows = jnp.concatenate(blocks, axis=0)
        columns += rows.shape[1]
        for h in range(2):
            product = jnp.dot(rows, panel(k, h), preferred_element_type=jnp.float32)
            totals[h] = product if k == 0 else totals[h] + product
        for r in range(tiles):
            wide = blocks[r].astype(jnp.float32)
            squares[r] += jnp.sum(wide * wide, axis=-1, keepdims=True)
    scale = lax.rsqrt(jnp.concatenate(squares, axis=0) / columns + epsilon)
    for h in range(2):
        total = totals[h] * scale
        lanes = slice(h * head_dim, (h + 1) * head_dim)
        q_ref[:, lanes] = rms_scale(total[:, :head_dim], query_gain_ref[...]).astype(jnp.bfloat16)
        k_ref[:, lanes] = rms_scale(
            total[:, head_dim : 2 * head_dim], key_gain_ref[...]
        ).astype(jnp.bfloat16)
        v_ref[:, lanes] = total[:, 2 * head_dim :].astype(jnp.bfloat16)


def attend_rows(pair, start, pos_ref, q_ref, k_ref, v_ref, held, mixed_ref):
    head_dim = q_ref.shape[1] // 2
    tile = mixed_ref.shape[0] // 2
    across = (((1,), (1,)), ((), ()))
    for h in range(2):
        for r in range(2 * pair, 2 * pair + 2):
            at = (r - 2 * pair) * tile
            rows = slice(start + at, start + at + tile)
            lanes = slice(h * head_dim, (h + 1) * head_dim)
            value_lanes = slice((2 + h) * head_dim, (3 + h) * head_dim)
            query = q_ref[rows, lanes]
            keys = [k_ref[rows, lanes]]
            values = [v_ref[rows, lanes]]
            for k in range(WAYS):
                block = pl.ds(pl.multiple_of(pos_ref[r * WAYS + k] * BLOCK, BLOCK), BLOCK)
                keys.append(held[k][block, lanes])
                values.append(held[k][block, value_lanes])
            key, value = jnp.concatenate(keys, axis=0), jnp.concatenate(values, axis=0)
            scores = lax.dot_general(query, key, across, preferred_element_type=jnp.float32)
            weights = jnp.exp(scores * head_dim ** (-0.5))
            total = jnp.sum(weights, axis=-1, keepdims=True)
            summed = jnp.dot(
                weights.astype(jnp.bfloat16), value, preferred_element_type=jnp.float32
            )
            mixed_ref[at : at + tile, lanes] = (summed / total).astype(jnp.bfloat16)


def project_kernel(source_ref, query_gain_ref, key_gain_ref, gathered_ref, *refs):
    panels, outs = refs[: 2 * WAYS], refs[2 * WAYS :]

    def part(j, k):
        return gathered_ref[source_ref[j * WAYS + k]]

    def panel(k, h):
        return panels[2 * k + h][...]

    project_rows(WAYS, part, panel, query_gain_ref, key_gain_ref, outs)


def attend_kernel(pair, pos_ref, q_ref, k_ref, v_ref, *refs):
    start = pair * refs[WAYS].shape[0]
    attend_rows(pair, start, pos_ref, q_ref, k_ref, v_ref, refs[:WAYS], refs[WAYS])


def mix_rows(pair, places, parts, panel, held, pos_ref, query_gain_ref, key_gain_ref, outs, mixed_ref):
    count = len(parts) // 2

    def part(j, k):
        at, inner = places[k]
        return parts[j * count + at][inner]

    project_rows(2, part, panel, query_gain_ref, key_gain_ref, outs)
    attend_rows(pair, 0, pos_ref, *outs, held(), mixed_ref)


def mix_own_kernel(places, pos_ref, query_gain_ref, key_gain_ref, *refs):
    parts, panels, caches = refs[:WAYS], refs[WAYS : 3 * WAYS], refs[3 * WAYS : 4 * WAYS]
    mixed_ref, panel_ref, held_ref, *outs, panel_sems, held_sems = refs[4 * WAYS :]
    copies = [
        pltpu.make_async_copy(source, panel_ref.at[i], panel_sems.at[i])
        for i, source in enumerate(panels)
    ]
    late = [
        pltpu.make_async_copy(source, held_ref.at[i], held_sems.at[i])
        for i, source in enumerate(caches)
    ]
    for copy in copies + late:
        copy.start()

    def panel(k, h):
        copies[2 * k + h].wait()
        return panel_ref[2 * k + h]

    def held():
        for copy in late:
            copy.wait()
        return [held_ref.at[k] for k in range(WAYS)]

    mix_rows(0, places, parts, panel, held, pos_ref, query_gain_ref, key_gain_ref, outs, mixed_ref)


def mix_other_kernel(places, pos_ref, query_gain_ref, key_gain_ref, *refs):
    *parts, panel_ref, held_ref, mixed_ref, q_ref, k_ref, v_ref = refs

    def panel(k, h):
        return panel_ref[2 * k + h]

    def held():
        return [held_ref.at[k] for k in range(WAYS)]

    outs = (q_ref, k_ref, v_ref)
    mix_rows(1, places, parts, panel, held, pos_ref, query_gain_ref, key_gain_ref, outs, mixed_ref)


def project(source, gains, gathered, panels):
    tile, head_dim = gathered.shape[1], gains[0].shape[1]
    return pl.pallas_call(
        project_kernel,
        out_shape=[jax.ShapeDtypeStruct((WAYS * tile, 2 * head_dim), jnp.bfloat16)] * 3,
        in_specs=[pl.BlockSpec(memory_space=pltpu.SMEM)] + whole_specs(3 + len(panels)),
        out_specs=whole_specs(3),
        compiler_params=pltpu.CompilerParams(vmem_limit_bytes=14 * MIB),
    )(source, *gains, gathered, *panels)


def attend_pair(pair, pos, qkv, held):
    rows, columns = qkv[0].shape
    return pl.pallas_call(
        functools.partial(attend_kernel, pair),
        out_shape=jax.ShapeDtypeStruct((rows // 2, columns), jnp.bfloat16),
        in_specs=[pl.BlockSpec(memory_space=pltpu.SMEM)] + whole_specs(3 + len(held)),
        out_specs=whole_specs(1)[0],
        compiler_params=pltpu.CompilerParams(vmem_limit_bytes=10 * MIB),
    )(pos, *qkv, *held)


def mix_own(places, pos, gains, parts, panels, held):
    tile, head_dim = parts[0].shape[1], gains[0].shape[1]
    shape = (2 * tile, 2 * head_dim)
    return pl.pallas_call(
        functools.partial(mix_own_kernel, places),
        out_shape=[
            jax.ShapeDtypeStruct(shape, jnp.bfloat16),
            jax.ShapeDtypeStruct((len(panels), *panels[0].shape), jnp.bfloat16),
            jax.ShapeDtypeStruct((len(held), *held[0].shape), jnp.bfloat16),
        ],
        in_specs=[pl.BlockSpec(memory_space=pltpu.SMEM)]
        + whole_specs(2 + len(parts))
        + [HBM_SPEC] * (len(panels) + len(held)),
        out_specs=whole_specs(3),
        scratch_shapes=[
            *[pltpu.VMEM(shape, jnp.bfloat16)] * 3,
            pltpu.SemaphoreType.DMA((len(panels),)),
            pltpu.SemaphoreType.DMA((len(held),)),
        ],
        compiler_params=pltpu.CompilerParams(vmem_limit_bytes=16 * MIB),
    )(pos, *gains, *parts, *map(in_hbm, panels), *map(in_hbm, held))


def mix_other(places, pos, gains, parts, panels, held):
    tile, head_dim = parts[0].shape[1], gains[0].shape[1]
    shape = (2 * tile, 2 * head_dim)
    return pl.pallas_call(
        functools.partial(mix_other_kernel, places),
        out_shape=jax.ShapeDtypeStruct(shape, jnp.bfloat16),
        in_specs=[pl.BlockSpec(memory_space=pltpu.SMEM)] + whole_specs(4 + len(parts)),
        out_specs=whole_specs(1)[0],
        scratch_shapes=[pltpu.VMEM(shape, jnp.bfloat16)] * 3,
        compiler_params=pltpu.CompilerParams(vmem_limit_bytes=16 * MIB),
    )(pos, *gains, *parts, panels, held)


def out_kernel(w_ref, *refs):
    mixed, (keep_ref, send_ref) = refs[:WAYS], refs[WAYS:]
    tile = keep_ref.shape[0]
    rows = jnp.concatenate([part[...] for part in mixed], axis=1)
    update = jnp.dot(rows, w_ref[...], preferred_element_type=jnp.float32)
    keep_ref[...] = update[:tile]
    send_ref[...] = update[tile:].astype(jnp.bfloat16)


def project_out(w_rows, mixed):
    shape = (mixed[0].shape[0] // 2, w_rows.shape[1])
    return pl.pallas_call(
        out_kernel,
        out_shape=[
            jax.ShapeDtypeStruct(shape, jnp.float32),
            jax.ShapeDtypeStruct(shape, jnp.bfloat16),
        ],
        in_specs=whole_specs(1 + WAYS),
        out_specs=whole_specs(2),
        compiler_params=pltpu.CompilerParams(vmem_limit_bytes=6 * MIB),
    )(w_rows, *mixed)


SWAP = [(0, 1), (1, 0)]


def from_z(value, k):
    return lax.ppermute(value, "cache", [(i, i ^ k) for i in range(WAYS)])


def split_heads(
    tokens,
    norm_gain,
    w_query,
    w_key,
    w_value,
    w_out,
    query_gain,
    key_gain,
    cache_keys,
    cache_values,
    step_gate,
    block_list,
    block_home,
    reader_span,
):
    z = lax.axis_index("cache")
    p = lax.axis_index(("fsdp", "head"))
    y = lax.axis_index("groups")
    head_dim = query_gain.shape[0]
    held_blocks = cache_keys.shape[0] // BLOCK
    width = tokens.shape[1] // WAYS
    tile = tokens.shape[0]
    ways = jnp.arange(WAYS, dtype=jnp.int32)

    def gather_pairs(by_z):
        low = jnp.stack(by_z[:2])
        low_x = lax.ppermute(low, "fsdp", SWAP)
        high = jnp.stack(by_z[2:])
        high_x = lax.ppermute(high, "fsdp", SWAP)
        mine = [low, high, low_x, high_x]
        low_c, high_c, low_xc, high_xc = [lax.ppermute(pair, "head", SWAP) for pair in mine]
        return [low, high, low_c, high_c, low_x, high_x, low_xc, high_xc]

    weights = (w_query, w_key, w_value)
    gain_lanes = jnp.broadcast_to(
        lax.dynamic_slice_in_dim(norm_gain, z * width, width, 0)[:, None], (width, head_dim)
    )
    order = (2, 3, 1)
    *sends, end = pack_panels([(k, 0) for k in order], gain_lanes, weights)
    sends = dict(zip(order, sends))
    near = {k: from_z(sends[k], k) for k in order}
    tokens, _ = lax.optimization_barrier((tokens, end))
    piece = lax.dynamic_slice_in_dim(tokens, p * width, width, 1)
    far_piece = from_z(piece, 2)
    parts = gather_pairs([piece, from_z(piece, 1), far_piece, from_z(far_piece, 1)])
    far = {k: lax.ppermute(near[k], "groups", SWAP) for k in order}
    packs = dict(zip((2, 3, 1, 0), pack_cache((2, 3, 1, 0), cache_keys, cache_values, head_dim)))
    held = [packs[0]]
    for k in range(1, WAYS):
        pack, _ = lax.optimization_barrier((packs[k], near[k]))
        held.append(from_z(pack, k))
    near[0], far[0], _ = pack_panels([(0, 0), (0, 1)], gain_lanes, weights)
    panels = [side[k] for k in range(WAYS) for side in (near, far)]
    gathered = jnp.concatenate(parts, axis=0)
    source = (z ^ p ^ ways)[None, :] * WAYS + (z ^ p ^ ways)[:, None]
    source = source.reshape(-1)
    x_share = lax.dynamic_index_in_dim(gathered, source[0], 0, keepdims=False)
    gains = (query_gain[None], key_gain[None])

    heads = jnp.stack([(z ^ ways) * 2 + y, (z ^ ways) * 2 + 1 - y], axis=1).reshape(-1)
    w_rows = jnp.take(w_out.reshape(2 * WAYS, head_dim, width), heads, axis=0).reshape(-1, width)
    gates = lax.dynamic_slice_in_dim(step_gate, z * width, width, 1)
    slots = jnp.take(block_home, jnp.take(block_list, jnp.take(reader_span, p ^ ways), axis=0))
    from_k = slots[:, :, None] // held_blocks == (z ^ ways)[None, None, :]
    pos = jnp.sum(jnp.where(from_k, (slots % held_blocks)[:, :, None], 0), axis=1).reshape(-1)

    def gather_z(own):
        near, far = lax.optimization_barrier((from_z(own, 1), from_z(own, 2)))
        return [own, near, far, from_z(far, 1)]

    def summed(mixed):
        keep, send = project_out(w_rows, mixed)
        return keep + lax.ppermute(send, "head", SWAP).astype(jnp.float32)

    qkv = project(source, gains, gathered, panels)
    mixed = gather_z(attend_pair(1, pos, qkv, held))
    pos_late, _ = lax.optimization_barrier((pos, mixed[0]))
    late = gather_z(attend_pair(0, pos_late, qkv, held))
    mixed[3], late[1], late[2] = lax.optimization_barrier((mixed[3], late[1], late[2]))
    other = summed(mixed).astype(jnp.bfloat16)
    other, late[3] = lax.optimization_barrier((other, late[3]))
    other = lax.ppermute(other, "fsdp", SWAP)
    update = summed(late) + other.astype(jnp.float32)
    x_share = (x_share.astype(jnp.float32) + gates[0] * update).astype(jnp.bfloat16)

    near, far, own_x = lax.optimization_barrier(
        (from_z(x_share, 1), from_z(x_share, 2), lax.ppermute(x_share[None], "fsdp", SWAP))
    )
    last = from_z(far, 1)
    by_z = [jnp.stack([x_share, near]), jnp.stack([far, last])]
    by_z += [lax.ppermute(part, "head", SWAP) for part in by_z]
    by_x = [own_x, *[lax.ppermute(v, "fsdp", SWAP) for v in (jnp.stack([near, far]), last[None])]]
    places = ((0, 0), (0, 1), (1, 0), (1, 1))
    own, panels, held = mix_own(places, pos, gains, by_z, panels, held)
    first = gather_z(own)
    by_x[1], by_x[2], first[0] = lax.optimization_barrier((by_x[1], by_x[2], first[0]))
    by_x += [lax.ppermute(part, "head", SWAP) for part in by_x]
    places = ((0, 0), (1, 0), (1, 1), (2, 0))
    second = gather_z(mix_other(places, pos, gains, by_x, panels, held))
    values = [x_share.astype(jnp.float32) + gates[1] * summed(first), gates[1] * summed(second)]
    ends = [
        lax.ppermute(
            value.astype(jnp.bfloat16),
            ("cache", "fsdp", "head"),
            [(a * WAYS + b, (b ^ flip) * WAYS + a) for a in range(WAYS) for b in range(WAYS)],
        ).astype(jnp.float32)
        for value, flip in zip(values, (0, 2))
    ]
    return (ends[0] + ends[1]).astype(jnp.bfloat16)


def solution(mesh):
    in_specs = (
        P(("groups", "cache"), None),
        P(),
        P("cache", ("fsdp", "head")),
        P("cache", ("fsdp", "head")),
        P("cache", ("fsdp", "head")),
        P(("fsdp", "head"), "cache"),
        P(),
        P(),
        P(("groups", "cache"), ("fsdp", "head")),
        P(("groups", "cache"), ("fsdp", "head")),
        P(),
        P("groups", None),
        P("groups"),
        P("groups"),
    )
    out_specs = P(("groups", "cache"), ("fsdp", "head"))
    sizes = dict(mesh.shape)

    def program(*args):
        panel_width, head_dim = args[2].shape[1] // (sizes["fsdp"] * sizes["head"]), args[6].shape[0]
        fits = (
            sizes == {"groups": 2, "cache": WAYS, "fsdp": 2, "head": 2}
            and panel_width == 2 * WAYS * head_dim
            and args[11].shape[1] == WAYS
            and ITERS == 2
        )
        plan = split_heads if fits else gathered_panels
        return jax.shard_map(
            plan, mesh=mesh, in_specs=in_specs, out_specs=out_specs, check_vma=False
        )(*args)

    return program
```

```python
import functools

import jax
import jax.numpy as jnp
from jax import lax
from jax.experimental import pallas as pl
from jax.experimental.pallas import tpu as pltpu
from jax.sharding import PartitionSpec as P

BLOCK = 256
ITERS = 2


epsilon = 1e-06


def rms_scale(values, gain_row):
    mean_square = jnp.mean(values * values, axis=-1, keepdims=True)
    return values * lax.rsqrt(mean_square + epsilon) * gain_row


def head_norm(projected, gain_row):
    row_count = projected.shape[0]
    split = projected.reshape(row_count, -1, gain_row.shape[0])
    return rms_scale(split, gain_row).astype(jnp.bfloat16).reshape(row_count, -1)


def attend(queries, key_rows, value_rows, head_dim):
    row_count = queries.shape[0]
    head_count = queries.shape[1] // head_dim
    query_heads = queries.reshape(row_count, head_count, head_dim)
    key_heads = key_rows.reshape(-1, head_count, head_dim)
    value_heads = value_rows.reshape(-1, head_count, head_dim)
    scores = jnp.einsum(
        "qhd,khd->hqk", query_heads, key_heads, preferred_element_type=jnp.float32
    ) * head_dim ** (-0.5)
    weights = jnp.exp(scores)
    totals = jnp.sum(weights, axis=2)
    summed = jnp.einsum(
        "hqk,khd->qhd",
        weights.astype(jnp.bfloat16),
        value_heads,
        preferred_element_type=jnp.float32,
    )
    return (
        (summed / jnp.transpose(totals)[:, :, None])
        .astype(jnp.bfloat16)
        .reshape(row_count, head_count * head_dim)
    )


def gathered_panels(
    tokens,
    norm_gain,
    w_query,
    w_key,
    w_value,
    w_out,
    query_gain,
    key_gain,
    cache_keys,
    cache_values,
    step_gate,
    block_list,
    block_home,
    reader_span,
):
    reader_index = lax.axis_index("cache")
    group_index = lax.axis_index(("fsdp", "head"))
    head_dim = query_gain.shape[0]
    panel_width = cache_keys.shape[1]
    held_blocks = cache_keys.shape[0] // BLOCK
    full_query, full_key, full_value = (
        lax.all_gather(w_query, "cache", axis=0, tiled=True),
        lax.all_gather(w_key, "cache", axis=0, tiled=True),
        lax.all_gather(w_value, "cache", axis=0, tiled=True),
    )
    out_panel = lax.all_gather(w_out, "cache", axis=1, tiled=True)
    wanted = jnp.take(block_list, reader_span, axis=0)
    home_slots = jnp.take(block_home, wanted)
    is_mine = home_slots // held_blocks == reader_index
    local_pos = jnp.sum(jnp.where(is_mine, home_slots % held_blocks, 0), axis=1)
    key_blocks = cache_keys.reshape(held_blocks, BLOCK, panel_width)
    value_blocks = cache_values.reshape(held_blocks, BLOCK, panel_width)
    send_keys = jnp.take(key_blocks, local_pos, axis=0)
    send_values = jnp.take(value_blocks, local_pos, axis=0)
    got_keys, got_values = (
        lax.all_to_all(send_keys, "cache", split_axis=0, concat_axis=0, tiled=True),
        lax.all_to_all(send_values, "cache", split_axis=0, concat_axis=0, tiled=True),
    )
    my_span = jnp.take(reader_span, reader_index)
    my_owners = jnp.take(block_home, jnp.take(block_list, my_span, axis=0)) // held_blocks
    fetched_keys = jnp.take(got_keys, my_owners, axis=0).reshape(-1, panel_width)
    fetched_values = jnp.take(got_values, my_owners, axis=0).reshape(-1, panel_width)
    out_columns = lax.all_to_all(
        out_panel, ("fsdp", "head"), split_axis=1, concat_axis=0, tiled=True
    )
    column_count = tokens.shape[1] // lax.axis_size(("fsdp", "head"))
    column_start = group_index * column_count
    current = tokens
    x_share = lax.dynamic_slice_in_dim(tokens, column_start, column_count, 1)
    for step_index in range(ITERS):
        normed = rms_scale(current.astype(jnp.float32), norm_gain).astype(jnp.bfloat16)
        queries = head_norm(
            jnp.dot(normed, full_query, preferred_element_type=jnp.float32), query_gain
        )
        own_keys = head_norm(
            jnp.dot(normed, full_key, preferred_element_type=jnp.float32), key_gain
        )
        own_values = jnp.dot(normed, full_value, preferred_element_type=jnp.float32).astype(
            jnp.bfloat16
        )
        all_keys = jnp.concatenate([fetched_keys, own_keys], axis=0)
        all_values = jnp.concatenate([fetched_values, own_values], axis=0)
        mixed = attend(queries, all_keys, all_values, head_dim)
        step_scale = step_gate[step_index]
        share_scale = lax.dynamic_slice_in_dim(step_scale, column_start, column_count, 0)
        heads_all = lax.all_gather(mixed, ("fsdp", "head"), axis=1, tiled=True)
        update = jnp.dot(heads_all, out_columns, preferred_element_type=jnp.float32)
        x_share = (x_share.astype(jnp.float32) + share_scale * update).astype(jnp.bfloat16)
        if step_index + 1 < ITERS:
            current = lax.all_gather(x_share, ("fsdp", "head"), axis=1, tiled=True)
    return x_share


WAYS = 4
MIB = 1024 * 1024


def in_hbm(value):
    return pltpu.with_memory_space_constraint(value, pltpu.HBM)


HBM_SPEC = pl.BlockSpec(memory_space=pltpu.HBM)


def whole_specs(count):
    return [pl.BlockSpec(memory_space=pltpu.VMEM) for _ in range(count)]


def head_lanes(k, h, head_dim):
    z, y = lax.axis_index("cache"), lax.axis_index("groups")
    return pl.ds(pl.multiple_of(((z ^ k) * 2 + (y ^ h)) * head_dim, head_dim), head_dim)


def pack_panels_kernel(slots, gain_ref, *refs):
    weights, panels, (end_ref, held_ref, sems) = refs[:3], refs[3:-3], refs[-3:]
    end_ref[...] = jnp.zeros_like(end_ref)
    head_dim = gain_ref.shape[1]
    copies = []
    for i, (k, h) in enumerate(slots):
        for m, weight in enumerate(weights):
            copies.append(
                pltpu.make_async_copy(
                    weight.at[:, head_lanes(k, h, head_dim)],
                    held_ref.at[i, :, m * head_dim : (m + 1) * head_dim],
                    sems.at[i * 3 + m],
                )
            )
            copies[-1].start()
    for i, panel in enumerate(panels):
        for m in range(3):
            copies[i * 3 + m].wait()
            lanes = slice(m * head_dim, (m + 1) * head_dim)
            panel[:, lanes] = (held_ref[i, :, lanes].astype(jnp.float32) * gain_ref[...]).astype(
                jnp.bfloat16
            )


def pack_panels(slots, gain_lanes, weights):
    depth, head_dim = gain_lanes.shape
    shape = jax.ShapeDtypeStruct((depth, 3 * head_dim), jnp.bfloat16)
    return pl.pallas_call(
        functools.partial(pack_panels_kernel, slots),
        out_shape=[shape] * len(slots) + [jax.ShapeDtypeStruct((8, head_dim), jnp.float32)],
        in_specs=whole_specs(1) + [HBM_SPEC] * 3,
        out_specs=whole_specs(len(slots) + 1),
        scratch_shapes=[
            pltpu.VMEM((len(slots), depth, 3 * head_dim), jnp.bfloat16),
            pltpu.SemaphoreType.DMA((3 * len(slots),)),
        ],
        compiler_params=pltpu.CompilerParams(vmem_limit_bytes=10 * MIB),
    )(gain_lanes, *[in_hbm(w) for w in weights])


def pack_cache_kernel(ks, keys_ref, values_ref, *refs):
    packs, sems = refs[:-1], refs[-1]
    head_dim = packs[0].shape[1] // 4
    copies = []
    for i, (k, pack) in enumerate(zip(ks, packs)):
        for m in range(4):
            source = (keys_ref, values_ref)[m // 2]
            copies.append(
                pltpu.make_async_copy(
                    source.at[:, head_lanes(k, m % 2, head_dim)],
                    pack.at[:, m * head_dim : (m + 1) * head_dim],
                    sems.at[i * 4 + m],
                )
            )
            copies[-1].start()
    for copy in copies:
        copy.wait()


def pack_cache(ks, keys, values, head_dim):
    shape = jax.ShapeDtypeStruct((keys.shape[0], 4 * head_dim), jnp.bfloat16)
    return pl.pallas_call(
        functools.partial(pack_cache_kernel, ks),
        out_shape=[shape] * len(ks),
        in_specs=[HBM_SPEC] * 2,
        out_specs=whole_specs(len(ks)),
        scratch_shapes=[pltpu.SemaphoreType.DMA((4 * len(ks),))],
        compiler_params=pltpu.CompilerParams(vmem_limit_bytes=6 * MIB),
    )(*map(in_hbm, (keys, values)))


def project_rows(tiles, part, panel, query_gain_ref, key_gain_ref, outs):
    q_ref, k_ref, v_ref = outs
    head_dim = query_gain_ref.shape[1]
    totals = [None, None]
    squares = [0.0] * tiles
    columns = 0
    wide_rows = []
    for k in range(WAYS):
        blocks = [part(r, k) for r in range(tiles)]
        rows = jnp.concatenate(blocks, axis=0)
        columns += rows.shape[1]
        wide_rows.append(rows)
        if callable(panel):
            for h in range(2):
                product = jnp.dot(rows, panel(k, h), preferred_element_type=jnp.float32)
                totals[h] = product if k == 0 else totals[h] + product
        for r in range(tiles):
            wide = blocks[r].astype(jnp.float32)
            squares[r] += jnp.sum(wide * wide, axis=-1, keepdims=True)
    if not callable(panel):
        rows = jnp.concatenate(wide_rows, axis=1)
        product = jnp.dot(rows, panel[...], preferred_element_type=jnp.float32)
        totals = [product[:, : 3 * head_dim], product[:, 3 * head_dim :]]
    scale = lax.rsqrt(jnp.concatenate(squares, axis=0) / columns + epsilon)
    for h in range(2):
        total = totals[h] * scale
        lanes = slice(h * head_dim, (h + 1) * head_dim)
        q_ref[:, lanes] = rms_scale(total[:, :head_dim], query_gain_ref[...]).astype(jnp.bfloat16)
        k_ref[:, lanes] = rms_scale(
            total[:, head_dim : 2 * head_dim], key_gain_ref[...]
        ).astype(jnp.bfloat16)
        v_ref[:, lanes] = total[:, 2 * head_dim :].astype(jnp.bfloat16)


def attend_rows(pair, start, pos_ref, q_ref, k_ref, v_ref, held, mixed_ref):
    head_dim = q_ref.shape[1] // 2
    tile = mixed_ref.shape[0] // 2
    across = (((1,), (1,)), ((), ()))
    for h in range(2):
        for r in range(2 * pair, 2 * pair + 2):
            at = (r - 2 * pair) * tile
            rows = slice(start + at, start + at + tile)
            lanes = slice(h * head_dim, (h + 1) * head_dim)
            value_lanes = slice((2 + h) * head_dim, (3 + h) * head_dim)
            query = q_ref[rows, lanes]
            keys = [k_ref[rows, lanes]]
            values = [v_ref[rows, lanes]]
            for k in range(WAYS):
                block = pl.ds(pl.multiple_of(pos_ref[r * WAYS + k] * BLOCK, BLOCK), BLOCK)
                keys.append(held[k][block, lanes])
                values.append(held[k][block, value_lanes])
            key, value = jnp.concatenate(keys, axis=0), jnp.concatenate(values, axis=0)
            scores = lax.dot_general(query, key, across, preferred_element_type=jnp.float32)
            weights = jnp.exp(scores * head_dim ** (-0.5))
            total = jnp.sum(weights, axis=-1, keepdims=True)
            summed = jnp.dot(
                weights.astype(jnp.bfloat16), value, preferred_element_type=jnp.float32
            )
            mixed_ref[at : at + tile, lanes] = (summed / total).astype(jnp.bfloat16)


def project_kernel(source_ref, query_gain_ref, key_gain_ref, gathered_ref, *refs):
    panels, outs = refs[: 2 * WAYS], refs[2 * WAYS :]

    def part(j, k):
        return gathered_ref[source_ref[j * WAYS + k]]

    def panel(k, h):
        return panels[2 * k + h][...]

    project_rows(WAYS, part, panel, query_gain_ref, key_gain_ref, outs)


def attend_kernel(pair, pos_ref, q_ref, k_ref, v_ref, *refs):
    start = pair * refs[WAYS].shape[0]
    attend_rows(pair, start, pos_ref, q_ref, k_ref, v_ref, refs[:WAYS], refs[WAYS])


def mix_rows(pair, places, parts, panel, held, pos_ref, query_gain_ref, key_gain_ref, outs, mixed_ref):
    count = len(parts) // 2

    def part(j, k):
        at, inner = places[k]
        return parts[j * count + at][inner]

    project_rows(2, part, panel, query_gain_ref, key_gain_ref, outs)
    attend_rows(pair, 0, pos_ref, *outs, held(), mixed_ref)


def mix_own_kernel(places, pos_ref, query_gain_ref, key_gain_ref, *refs):
    parts, panels, caches = refs[:WAYS], refs[WAYS : 3 * WAYS], refs[3 * WAYS : 4 * WAYS]
    mixed_ref, panel_ref, held_ref, *outs, panel_sems, held_sems = refs[4 * WAYS :]
    depth, lanes = panels[0].shape
    copies = [
        pltpu.make_async_copy(
            source,
            panel_ref.at[
                i // 2 * depth : (i // 2 + 1) * depth, i % 2 * lanes : (i % 2 + 1) * lanes
            ],
            panel_sems.at[i],
        )
        for i, source in enumerate(panels)
    ]
    late = [
        pltpu.make_async_copy(source, held_ref.at[i], held_sems.at[i])
        for i, source in enumerate(caches)
    ]
    for copy in copies + late:
        copy.start()

    def panel(k, h):
        copies[2 * k + h].wait()
        return panel_ref[k * depth : (k + 1) * depth, h * lanes : (h + 1) * lanes]

    def held():
        for copy in late:
            copy.wait()
        return [held_ref.at[k] for k in range(WAYS)]

    mix_rows(0, places, parts, panel, held, pos_ref, query_gain_ref, key_gain_ref, outs, mixed_ref)


def mix_other_kernel(places, pos_ref, query_gain_ref, key_gain_ref, *refs):
    *parts, panel_ref, held_ref, mixed_ref, q_ref, k_ref, v_ref = refs

    panel = panel_ref

    def held():
        return [held_ref.at[k] for k in range(WAYS)]

    outs = (q_ref, k_ref, v_ref)
    mix_rows(1, places, parts, panel, held, pos_ref, query_gain_ref, key_gain_ref, outs, mixed_ref)


def project(source, gains, gathered, panels):
    tile, head_dim = gathered.shape[1], gains[0].shape[1]
    return pl.pallas_call(
        project_kernel,
        out_shape=[jax.ShapeDtypeStruct((WAYS * tile, 2 * head_dim), jnp.bfloat16)] * 3,
        in_specs=[pl.BlockSpec(memory_space=pltpu.SMEM)] + whole_specs(3 + len(panels)),
        out_specs=whole_specs(3),
        compiler_params=pltpu.CompilerParams(vmem_limit_bytes=14 * MIB),
    )(source, *gains, gathered, *panels)


def attend_pair(pair, pos, qkv, held):
    rows, columns = qkv[0].shape
    return pl.pallas_call(
        functools.partial(attend_kernel, pair),
        out_shape=jax.ShapeDtypeStruct((rows // 2, columns), jnp.bfloat16),
        in_specs=[pl.BlockSpec(memory_space=pltpu.SMEM)] + whole_specs(3 + len(held)),
        out_specs=whole_specs(1)[0],
        compiler_params=pltpu.CompilerParams(vmem_limit_bytes=10 * MIB),
    )(pos, *qkv, *held)


def mix_own(places, pos, gains, parts, panels, held):
    tile, head_dim = parts[0].shape[1], gains[0].shape[1]
    shape = (2 * tile, 2 * head_dim)
    return pl.pallas_call(
        functools.partial(mix_own_kernel, places),
        out_shape=[
            jax.ShapeDtypeStruct(shape, jnp.bfloat16),
            jax.ShapeDtypeStruct((WAYS * panels[0].shape[0], 2 * panels[0].shape[1]), jnp.bfloat16),
            jax.ShapeDtypeStruct((len(held), *held[0].shape), jnp.bfloat16),
        ],
        in_specs=[pl.BlockSpec(memory_space=pltpu.SMEM)]
        + whole_specs(2 + len(parts))
        + [HBM_SPEC] * (len(panels) + len(held)),
        out_specs=whole_specs(3),
        scratch_shapes=[
            *[pltpu.VMEM(shape, jnp.bfloat16)] * 3,
            pltpu.SemaphoreType.DMA((len(panels),)),
            pltpu.SemaphoreType.DMA((len(held),)),
        ],
        compiler_params=pltpu.CompilerParams(vmem_limit_bytes=16 * MIB),
    )(pos, *gains, *parts, *map(in_hbm, panels), *map(in_hbm, held))


def mix_other(places, pos, gains, parts, panels, held):
    tile, head_dim = parts[0].shape[1], gains[0].shape[1]
    shape = (2 * tile, 2 * head_dim)
    return pl.pallas_call(
        functools.partial(mix_other_kernel, places),
        out_shape=jax.ShapeDtypeStruct(shape, jnp.bfloat16),
        in_specs=[pl.BlockSpec(memory_space=pltpu.SMEM)] + whole_specs(4 + len(parts)),
        out_specs=whole_specs(1)[0],
        scratch_shapes=[pltpu.VMEM(shape, jnp.bfloat16)] * 3,
        compiler_params=pltpu.CompilerParams(vmem_limit_bytes=16 * MIB),
    )(pos, *gains, *parts, panels, held)


def out_kernel(w_ref, *refs):
    mixed, (keep_ref, send_ref) = refs[:WAYS], refs[WAYS:]
    tile = keep_ref.shape[0]
    rows = jnp.concatenate([part[...] for part in mixed], axis=1)
    update = jnp.dot(rows, w_ref[...], preferred_element_type=jnp.float32)
    keep_ref[...] = update[:tile]
    send_ref[...] = update[tile:].astype(jnp.bfloat16)


def project_out(w_rows, mixed):
    shape = (mixed[0].shape[0] // 2, w_rows.shape[1])
    return pl.pallas_call(
        out_kernel,
        out_shape=[
            jax.ShapeDtypeStruct(shape, jnp.float32),
            jax.ShapeDtypeStruct(shape, jnp.bfloat16),
        ],
        in_specs=whole_specs(1 + WAYS),
        out_specs=whole_specs(2),
        compiler_params=pltpu.CompilerParams(vmem_limit_bytes=6 * MIB),
    )(w_rows, *mixed)


SWAP = [(0, 1), (1, 0)]


def from_z(value, k):
    return lax.ppermute(value, "cache", [(i, i ^ k) for i in range(WAYS)])


def split_heads(
    tokens,
    norm_gain,
    w_query,
    w_key,
    w_value,
    w_out,
    query_gain,
    key_gain,
    cache_keys,
    cache_values,
    step_gate,
    block_list,
    block_home,
    reader_span,
):
    z = lax.axis_index("cache")
    p = lax.axis_index(("fsdp", "head"))
    y = lax.axis_index("groups")
    head_dim = query_gain.shape[0]
    held_blocks = cache_keys.shape[0] // BLOCK
    width = tokens.shape[1] // WAYS
    tile = tokens.shape[0]
    ways = jnp.arange(WAYS, dtype=jnp.int32)

    def gather_pairs(by_z):
        low = jnp.stack(by_z[:2])
        low_x = lax.ppermute(low, "fsdp", SWAP)
        high = jnp.stack(by_z[2:])
        high_x = lax.ppermute(high, "fsdp", SWAP)
        mine = [low, high, low_x, high_x]
        low_c, high_c, low_xc, high_xc = [lax.ppermute(pair, "head", SWAP) for pair in mine]
        return [low, high, low_c, high_c, low_x, high_x, low_xc, high_xc]

    weights = (w_query, w_key, w_value)
    gain_lanes = jnp.broadcast_to(
        lax.dynamic_slice_in_dim(norm_gain, z * width, width, 0)[:, None], (width, head_dim)
    )
    order = (2, 3, 1)
    *sends, end = pack_panels([(k, 0) for k in order], gain_lanes, weights)
    sends = dict(zip(order, sends))
    near = {k: from_z(sends[k], k) for k in order}
    tokens, _ = lax.optimization_barrier((tokens, end))
    piece = lax.dynamic_slice_in_dim(tokens, p * width, width, 1)
    far_piece = from_z(piece, 2)
    parts = gather_pairs([piece, from_z(piece, 1), far_piece, from_z(far_piece, 1)])
    far = {k: lax.ppermute(near[k], "groups", SWAP) for k in order}
    packs = dict(zip((2, 3, 1, 0), pack_cache((2, 3, 1, 0), cache_keys, cache_values, head_dim)))
    held = [packs[0]]
    for k in range(1, WAYS):
        pack, _ = lax.optimization_barrier((packs[k], near[k]))
        held.append(from_z(pack, k))
    near[0], far[0], _ = pack_panels([(0, 0), (0, 1)], gain_lanes, weights)
    panels = [side[k] for k in range(WAYS) for side in (near, far)]
    gathered = jnp.concatenate(parts, axis=0)
    source = (z ^ p ^ ways)[None, :] * WAYS + (z ^ p ^ ways)[:, None]
    source = source.reshape(-1)
    x_share = lax.dynamic_index_in_dim(gathered, source[0], 0, keepdims=False)
    gains = (query_gain[None], key_gain[None])

    heads = jnp.stack([(z ^ ways) * 2 + y, (z ^ ways) * 2 + 1 - y], axis=1).reshape(-1)
    w_rows = jnp.take(w_out.reshape(2 * WAYS, head_dim, width), heads, axis=0).reshape(-1, width)
    gates = lax.dynamic_slice_in_dim(step_gate, z * width, width, 1)
    slots = jnp.take(block_home, jnp.take(block_list, jnp.take(reader_span, p ^ ways), axis=0))
    from_k = slots[:, :, None] // held_blocks == (z ^ ways)[None, None, :]
    pos = jnp.sum(jnp.where(from_k, (slots % held_blocks)[:, :, None], 0), axis=1).reshape(-1)

    def gather_z(own):
        near, far = lax.optimization_barrier((from_z(own, 1), from_z(own, 2)))
        return [own, near, far, from_z(far, 1)]

    def summed(mixed):
        keep, send = project_out(w_rows, mixed)
        return keep + lax.ppermute(send, "head", SWAP).astype(jnp.float32)

    qkv = project(source, gains, gathered, panels)
    mixed = gather_z(attend_pair(1, pos, qkv, held))
    pos_late, _ = lax.optimization_barrier((pos, mixed[0]))
    late = gather_z(attend_pair(0, pos_late, qkv, held))
    mixed[3], late[1], late[2] = lax.optimization_barrier((mixed[3], late[1], late[2]))
    other = summed(mixed).astype(jnp.bfloat16)
    other, late[3] = lax.optimization_barrier((other, late[3]))
    other = lax.ppermute(other, "fsdp", SWAP)
    update = summed(late) + other.astype(jnp.float32)
    x_share = (x_share.astype(jnp.float32) + gates[0] * update).astype(jnp.bfloat16)

    near, far, own_x = lax.optimization_barrier(
        (from_z(x_share, 1), from_z(x_share, 2), lax.ppermute(x_share[None], "fsdp", SWAP))
    )
    last = from_z(far, 1)
    by_z = [jnp.stack([x_share, near]), jnp.stack([far, last])]
    by_z += [lax.ppermute(part, "head", SWAP) for part in by_z]
    by_x = [own_x, *[lax.ppermute(v, "fsdp", SWAP) for v in (jnp.stack([near, far]), last[None])]]
    places = ((0, 0), (0, 1), (1, 0), (1, 1))
    own, panels, held = mix_own(places, pos, gains, by_z, panels, held)
    first = gather_z(own)
    by_x[1], by_x[2], first[0] = lax.optimization_barrier((by_x[1], by_x[2], first[0]))
    by_x += [lax.ppermute(part, "head", SWAP) for part in by_x]
    places = ((0, 0), (1, 0), (1, 1), (2, 0))
    second = gather_z(mix_other(places, pos, gains, by_x, panels, held))
    values = [x_share.astype(jnp.float32) + gates[1] * summed(first), gates[1] * summed(second)]
    ends = [
        lax.ppermute(
            value.astype(jnp.bfloat16),
            ("cache", "fsdp", "head"),
            [(a * WAYS + b, (b ^ flip) * WAYS + a) for a in range(WAYS) for b in range(WAYS)],
        ).astype(jnp.float32)
        for value, flip in zip(values, (0, 2))
    ]
    return (ends[0] + ends[1]).astype(jnp.bfloat16)


def solution(mesh):
    in_specs = (
        P(("groups", "cache"), None),
        P(),
        P("cache", ("fsdp", "head")),
        P("cache", ("fsdp", "head")),
        P("cache", ("fsdp", "head")),
        P(("fsdp", "head"), "cache"),
        P(),
        P(),
        P(("groups", "cache"), ("fsdp", "head")),
        P(("groups", "cache"), ("fsdp", "head")),
        P(),
        P("groups", None),
        P("groups"),
        P("groups"),
    )
    out_specs = P(("groups", "cache"), ("fsdp", "head"))
    sizes = dict(mesh.shape)

    def program(*args):
        panel_width, head_dim = args[2].shape[1] // (sizes["fsdp"] * sizes["head"]), args[6].shape[0]
        fits = (
            sizes == {"groups": 2, "cache": WAYS, "fsdp": 2, "head": 2}
            and panel_width == 2 * WAYS * head_dim
            and args[11].shape[1] == WAYS
            and ITERS == 2
        )
        plan = split_heads if fits else gathered_panels
        return jax.shard_map(
            plan, mesh=mesh, in_specs=in_specs, out_specs=out_specs, check_vma=False
        )(*args)

    return program
```
